512 devices in a mesh: section: 8 (over z_hi, core), seq: 64 (over z_lo, y, x).
Axes of the slice: x: 4, y: 4, z: 16 (z_hi: 4, z_lo: 4; z = z_hi * 4 + z_lo), core: 2. Of those that a mesh axis runs over, the one named last changes fastest.
Arguments:
- bases: int32 [2, 32768], P(None, 'seq'), may hold values from 0 to 3
- stem_weight: bfloat16 [15, 4, 1536], replicated, may hold values from -1.5 to 1.5
- gains: bfloat16 [8, 1536], P('section'), may hold values from 0.099609375 to 1.8984375
- depth_taps: bfloat16 [8, 5, 1536], P('section'), may hold values from -2.5 to 2.5
- point_weight: bfloat16 [8, 1536, 1536], P('section', 'seq'), may hold values from -0.15625 to 0.15625
Outputs:
- encoded: bfloat16 [2, 128, 1536], P(None, 'seq', 'section')
The draws below stay inside these ranges and needn't reach their ends.
All inputs are finite; a program needn't handle non-finite values.
Results may differ from the reference program's by a relative error of at most 0.015.
Values may be sent and summed in bfloat16 or wider, within the bound.
No kernel may reach another device: no remote copies, remote signals or barrier semaphores. Data moves between devices by JAX's collectives and lax.ppermute only.
A program may use at most 64 MiB of HBM per device.

```python
import jax
import jax.numpy as jnp
from jax import lax

C = 1536
K0 = 15
KERNEL_TAPS = 5
DILATION_STEP = 2
MB = 2
L0 = 32768
N_SECTION = 8


def place_ends(array, own_key, least, high):
    longest = array.shape.index(max(array.shape))
    spots = []
    for shift in (0, 1):
        where = [jax.random.randint(jax.random.fold_in(own_key, axis), (), 0, length) for axis, length in enumerate(array.shape)]
        where[longest] = (where[longest] + shift) % array.shape[longest]
        spots.append(tuple(where))
    return array.at[spots[0]].set(least).at[spots[1]].set(high)


def block_levels(rng, dims, shards, low, high):
    factor_of = 1.0
    for dim, blocks in shards:
        heights = jax.random.uniform(jax.random.fold_in(jax.random.fold_in(rng, 6), dim), (blocks,), jnp.float32, low / len(shards), high / len(shards))
        factor_of = factor_of * jnp.repeat(jnp.exp(heights), dims[dim] // blocks).reshape((-1,) + (1,) * (len(dims) - 1 - dim))
    return factor_of


def bell_draw(own_key, shape, deviation, limit, cuts=(), kind=jnp.bfloat16):
    values = deviation * jax.random.normal(own_key, shape, jnp.float32)
    if cuts:
        values = values * block_levels(own_key, shape, cuts, -0.22, 0.18)
    return jnp.clip(values, -limit, limit).astype(kind)


def setup_inputs(seed: int = 0) -> dict:
    splits = jax.random.split(jax.random.key(seed), 6)
    bases = place_ends(jax.random.randint(splits[0], (MB, L0), 0, 4), jax.random.fold_in(splits[0], 1), 0, 3).astype(jnp.int32)
    stem_weight = bell_draw(splits[1], (K0, 4, C), K0 ** -0.5, 1.5)
    gains = jnp.clip(1.0 + 0.18 * jax.random.normal(splits[2], (N_SECTION, C), jnp.float32), 0.099609375, 1.8984375).astype(jnp.bfloat16)
    depth_taps = bell_draw(splits[3], (N_SECTION, KERNEL_TAPS, C), KERNEL_TAPS ** -0.5, 2.5, ((0, 8),))
    point_weight = bell_draw(splits[4], (N_SECTION, C, C), C ** -0.5, 0.15625, ((0, 8), (1, 64)))
    return {"bases": bases, "stem_weight": stem_weight, "gains": gains, "depth_taps": depth_taps, "point_weight": point_weight}


def normalize_gelu(rows, gain_row):
    values = rows.astype(jnp.float32)
    square_mean = lax.optimization_barrier(jnp.mean(values * values, axis=-1, keepdims=True))
    scaled = values * lax.rsqrt(square_mean + 1e-06) * gain_row.astype(jnp.float32)
    return jax.nn.gelu(scaled, approximate=True).astype(jnp.bfloat16)

def filter_rows(extended_rows, kernel_weight, length_total):
    summed = jnp.zeros((length_total, extended_rows.shape[1]), jnp.float32)
    for offset_amount in range(kernel_weight.shape[0]):
        window_rows = extended_rows[offset_amount * DILATION_STEP:offset_amount * DILATION_STEP + length_total].astype(jnp.float32)
        summed = summed + kernel_weight[offset_amount].astype(jnp.float32) * window_rows
    return summed.astype(jnp.bfloat16)

def halve_rows(rows):
    return lax.optimization_barrier(jnp.max(rows.reshape(rows.shape[0] // 2, 2, rows.shape[1]), axis=1))

def stem_rows(extended_ids, stem_weight, length_total):
    one_hot = (extended_ids[:, None] == jnp.arange(1, 5, dtype=jnp.int32)[None, :]).astype(jnp.bfloat16)
    window_rows = jnp.concatenate([one_hot[offset_amount:offset_amount + length_total] for offset_amount in range(stem_weight.shape[0])], axis=1)
    flat = stem_weight.reshape(stem_weight.shape[0] * 4, stem_weight.shape[2])
    return jnp.dot(window_rows, flat, preferred_element_type=jnp.float32).astype(jnp.bfloat16)

def encode_one(sequence, stem_weight, gains, depth_taps, point_weight):
    margin = K0 // 2
    extended_ids = jnp.pad(sequence + 1, (margin, margin))
    current = stem_rows(extended_ids, stem_weight, sequence.shape[0])
    spread_width = KERNEL_TAPS // 2 * DILATION_STEP
    for level in range(N_SECTION):
        activated = normalize_gelu(current, gains[level])
        extended_rows = jnp.pad(activated, ((spread_width, spread_width), (0, 0)))
        filtered = filter_rows(extended_rows, depth_taps[level], current.shape[0])
        mixed_rows = (current.astype(jnp.float32) + jnp.dot(filtered, point_weight[level], preferred_element_type=jnp.float32)).astype(jnp.bfloat16)
        current = halve_rows(mixed_rows)
    return current

def reference(bases, stem_weight, gains, depth_taps, point_weight):
    outputs = []
    for sequence_index in range(MB):
        outputs.append(encode_one(bases[sequence_index], stem_weight, gains, depth_taps, point_weight))
    return jnp.stack(outputs)
```

```python
import jax
import jax.numpy as jnp
from jax import lax
from jax.experimental import pallas as pl
from jax.experimental.pallas import tpu as pltpu
from jax.sharding import Mesh
from jax.sharding import PartitionSpec as P


SEQ = ("zl", "y", "x")
SECTION = ("zh", "co")
C = 1536
HALF = C // 2
TAPS = 5
RUN = 1024
EDGE = 12
BLOCK = 96
SHIFTS = (0, 1, -1, 2)


def up16(rows):
    return -(-rows // 16) * 16


def activate(load, par_ref, a_scr, rows, edge, first, last):
    def step(i, carry):
        start = pl.multiple_of(i * 16, 16)
        left, right = load(start)
        squares = jnp.sum(left * left, axis=-1, keepdims=True)
        squares = squares + jnp.sum(right * right, axis=-1, keepdims=True)
        scale = lax.rsqrt(squares * (1.0 / C) + 1e-06)
        index = start + lax.broadcasted_iota(jnp.int32, (16, 1), 0)
        low = jnp.where(first == 1, edge, 0)
        high = jnp.where(last == 1, rows - edge, rows)
        inside = (index >= low) & (index < high)
        for side, part in enumerate((left, right)):
            lanes = pl.ds(side * HALF, HALF)
            value = part * scale * par_ref[0:1, lanes]
            value = jax.nn.gelu(value, approximate=True).astype(jnp.bfloat16)
            a_scr[pl.ds(start + 8, 16), lanes] = jnp.where(inside, value.astype(jnp.float32), 0.0)
        return carry

    lax.fori_loop(0, up16(rows) // 16, step, 0)


def spread(par_ref, a_scr, d_ref, rows):
    width = 384
    for lane in range(0, C, width):
        taps = [par_ref[1 + k : 2 + k, lane : lane + width] for k in range(TAPS)]

        def step(i, carry):
            start = pl.multiple_of(i * 16, 16)
            window = a_scr[pl.ds(start, 32), lane : lane + width]
            total = taps[0] * window[4:20]
            for k in range(1, TAPS):
                total = total + taps[k] * window[4 + 2 * k : 20 + 2 * k]
            d_ref[pl.ds(start, 16), lane : lane + width] = total.astype(jnp.bfloat16)
            return carry

        lax.fori_loop(0, up16(rows) // 16, step, 0)


def weight_copies(meta_ref, pieces, w_scr, sems):
    copies = []
    for p, piece in enumerate(pieces):
        for k in range(4):
            row = pl.multiple_of(meta_ref[3 + 4 * p + k] * BLOCK, 16)
            target = w_scr.at[pl.ds(row, BLOCK)]
            copies.append(pltpu.make_async_copy(piece.at[k], target, sems.at[4 * p + k]))
    return copies


def mix_and_pool(d_ref, w_scr, residual, y_scr, out_ref, rows, count):
    total = up16(rows)
    chunk = next(total // n for n in range(1, 99) if total % (16 * n) == 0 and total // n <= 272)
    for start in range(0, total, chunk):
        product = jnp.dot(
            d_ref[start : start + chunk], w_scr[...], preferred_element_type=jnp.float32
        )
        mixed = residual(start, chunk) + product
        for n in range(HALF // 128):
            y_scr[n, start : start + chunk] = mixed[:, 128 * n : 128 * n + 128]
    part = next(p for p in (128, 104, 64, 40, 16, 8, 4) if count % p == 0)
    for start in range(0, count, part):
        for n in range(HALF // 128):
            even = y_scr[n, pl.ds(4 + 2 * start, part, stride=2)]
            odd = y_scr[n, pl.ds(5 + 2 * start, part, stride=2)]
            pooled = jnp.maximum(even, odd).astype(jnp.bfloat16)
            out_ref[start : start + part, 128 * n : 128 * n + 128] = pooled


def first_half(rows, meta_ref, hot_ref, stem_ref, par_ref, x_ref, d_ref, x_scr, a_scr):
    chunk = 176
    for start in range(0, up16(rows), chunk):
        for side in range(2):
            x_scr[side, start : start + chunk] = jnp.dot(
                hot_ref[start : start + chunk],
                stem_ref[:, side * HALF : (side + 1) * HALF],
                preferred_element_type=jnp.float32,
            ).astype(jnp.bfloat16)

    def load(start):
        return [x_scr[side, pl.ds(start, 16)].astype(jnp.float32) for side in range(2)]

    activate(load, par_ref, a_scr, rows, EDGE, meta_ref[1], meta_ref[2])
    spread(par_ref, a_scr, d_ref, rows)
    x_ref[...] = x_scr[meta_ref[0]]


def second_half(rows, meta_ref, x_ref, d_ref, w0, w1, w2, w3, out_ref, w_scr, y_scr, sems):
    copies = weight_copies(meta_ref, (w0, w1, w2, w3), w_scr, sems)
    for copy in copies:
        copy.start()
    for copy in copies:
        copy.wait()

    def residual(start, chunk):
        return x_ref[start : start + chunk].astype(jnp.float32)

    mix_and_pool(d_ref, w_scr, residual, y_scr, out_ref, rows, (rows - 8) // 2)


def whole_level(
    rows, edge, meta_ref, x_ref, par_ref, w0, w1, w2, w3, out_ref, a_scr, d_scr, w_scr, y_scr, sems
):
    copies = weight_copies(meta_ref, (w0, w1, w2, w3), w_scr, sems)
    for copy in copies:
        copy.start()

    def load(start):
        return [x_ref[side, pl.ds(start, 16)].astype(jnp.float32) for side in range(2)]

    activate(load, par_ref, a_scr, rows, edge, meta_ref[1], meta_ref[2])
    spread(par_ref, a_scr, d_scr, rows)
    for copy in copies:
        copy.wait()

    def residual(start, chunk):
        return x_ref[meta_ref[0], start : start + chunk].astype(jnp.float32)

    mix_and_pool(d_scr, w_scr, residual, y_scr, out_ref, rows, (rows - 8) // 2)


def spec(memory_space=pltpu.VMEM):
    return pl.BlockSpec(memory_space=memory_space)


def out_rows(rows, last):
    return (rows - 8) // 2 if last else up16((rows - 8) // 2)


def run_first_half(rows, meta, hot, stem, par):
    size = up16(rows)
    return pl.pallas_call(
        lambda *refs: first_half(rows, *refs),
        in_specs=[spec(pltpu.SMEM), spec(), spec(), spec()],
        out_specs=[spec(), spec()],
        out_shape=[
            jax.ShapeDtypeStruct((size, HALF), jnp.bfloat16),
            jax.ShapeDtypeStruct((size, C), jnp.bfloat16),
        ],
        scratch_shapes=[
            pltpu.VMEM((2, size, HALF), jnp.bfloat16),
            pltpu.VMEM((size + 16, C), jnp.float32),
        ],
        name="stem_and_taps",
    )(meta, hot, stem, par)


def run_second_half(rows, meta, x, d, pieces):
    size = up16(rows)
    return pl.pallas_call(
        lambda *refs: second_half(rows, *refs),
        in_specs=[spec(pltpu.SMEM), spec(), spec()] + [spec(pl.ANY)] * 4,
        out_specs=spec(),
        out_shape=jax.ShapeDtypeStruct((out_rows(rows, False), HALF), jnp.bfloat16),
        scratch_shapes=[
            pltpu.VMEM((C, HALF), jnp.bfloat16),
            pltpu.VMEM((HALF // 128, size, 128), jnp.float32),
            pltpu.SemaphoreType.DMA((16,)),
        ],
        name="mix_first",
    )(meta, x, d, *pieces)


def run_level(rows, edge, last, meta, x, par, pieces):
    size = up16(rows)
    return pl.pallas_call(
        lambda *refs: whole_level(rows, edge, *refs),
        in_specs=[spec(pltpu.SMEM), spec(), spec()] + [spec(pl.ANY)] * 4,
        out_specs=spec(),
        out_shape=jax.ShapeDtypeStruct((out_rows(rows, last), HALF), jnp.bfloat16),
        scratch_shapes=[
            pltpu.VMEM((size + 16, C), jnp.float32),
            pltpu.VMEM((size, C), jnp.bfloat16),
            pltpu.VMEM((C, HALF), jnp.bfloat16),
            pltpu.VMEM((HALF // 128, size, 128), jnp.float32),
            pltpu.SemaphoreType.DMA((16,)),
        ],
        name=f"level_{rows}_{edge}",
    )(meta, x, par, *pieces)


def ring(size, by):
    return [(i, (i + by) % size) for i in range(size)]


def around(array, axes, size):
    return [array] + [lax.ppermute(array, axes, ring(size, by)) for by in SHIFTS[1:]]


def by_role(array, j):
    pairs = [
        (zs * 4 + x0, ((x0 - j) % 4) * 4 + zs) for zs in range(4) for x0 in range(4)
    ]
    return lax.ppermute(array, ("zh", "x"), pairs)


def flat(b, g, role):
    zh, zl, y = 2 * b + g % 2, g // 8, (g // 2) % 4
    return ((zh * 4 + zl) * 4 + y) * 4 + role


def pass_on(array, role):
    rows = array.shape[0]
    axes = ("zh", "zl", "y", "x")
    up = [(flat(b, g, role), flat(b, g + 1, role + 1)) for b in range(2) for g in range(31)]
    down = [(flat(b, g + 1, role), flat(b, g, role + 1)) for b in range(2) for g in range(31)]
    before = lax.ppermute(array[rows - EDGE :], axes, up)
    after = lax.ppermute(array[:EDGE], axes, down)
    own = lax.ppermute(array, "x", [(role, role + 1)])
    blank = jnp.zeros((8, HALF), array.dtype)
    return jnp.concatenate([before, own, after, blank], axis=0)


def shards(bases, stem_weight, gains, depth_taps, point_weight):
    zh, co, zl, y, x = [lax.axis_index(name) for name in ("zh", "co", "zl", "y", "x")]
    margin = stem_weight.shape[0] // 2
    group = (zl * 4 + y) * 2 + zh % 2
    sequence = zh // 2

    params = jnp.concatenate(
        [gains, depth_taps[0], jnp.zeros((2, C), gains.dtype)], axis=0
    )
    params = by_role(lax.all_gather(params, "co"), 0).astype(jnp.float32)
    own = point_weight[0].reshape(-1, 2, HALF).transpose(1, 0, 2)
    own = lax.all_to_all(own, "co", 0, 0, tiled=True)
    turned = jnp.stack([by_role(own, j) for j in range(4)] * 2, axis=0)
    ordered = lax.dynamic_slice_in_dim(turned, (4 - zh) % 4, 4, 0)
    blocks = [ordered[:, slot].reshape(BLOCK, HALF) for slot in range(2)]
    along_z = jnp.stack(around(blocks[0], ("zh", "zl"), 16))
    along_y = jnp.stack(around(blocks[1], "y", 4))
    weights = [around(along_z, "y", 4), around(along_y, ("zh", "zl"), 16)]
    shift = jnp.array(SHIFTS, jnp.int32)
    z_of, y_of = (zl - shift) % 4, (y - shift) % 4
    places = [
        (z_of[None, :] * 4 + y_of[:, None]).reshape(-1),
        (z_of[:, None] * 4 + y_of[None, :]).reshape(-1),
    ]
    flags = jnp.stack([co, (group == 0).astype(jnp.int32), (group == 31).astype(jnp.int32)])
    metas = [jnp.concatenate([flags.astype(jnp.int32), place]) for place in places]

    rows = RUN + 2 * EDGE
    copies = lax.optimization_barrier(jnp.broadcast_to((bases + 1)[None], (64, *bases.shape)))
    everywhere = lax.all_to_all(copies, SEQ, 0, 0, tiled=True)
    mine = lax.dynamic_index_in_dim(everywhere, sequence, 1, keepdims=False).reshape(-1)
    mine = jnp.pad(mine, (EDGE + margin, 64))
    size = up16(rows)
    ids = lax.dynamic_slice_in_dim(mine, group * RUN, size + 2 * margin, 0)
    hot = (ids[:, None] == jnp.arange(1, 5, dtype=jnp.int32)[None, :]).astype(jnp.bfloat16)
    windows = [hot[k : k + size] for k in range(2 * margin + 1)]
    windows = jnp.concatenate(windows + [jnp.zeros((size, 4), jnp.bfloat16)], axis=1)
    stem = jnp.pad(stem_weight.reshape(-1, C), ((0, 4), (0, 0)))
    level_rows, taps = run_first_half(rows, metas[0], windows, stem, params[0])
    now = run_second_half(rows, metas[0], level_rows, taps, weights[0])
    now = lax.all_gather(now, "co")
    now = run_level(RUN // 2 + 8, 4, True, metas[1], now, params[1], weights[1])
    run = RUN // 4
    for role in range(3):
        now = lax.all_gather(pass_on(now, role), "co")
        now = run_level(run + 2 * EDGE, EDGE, False, metas[0], now, params[0], weights[0])
        now = lax.all_gather(now, "co")
        now = run_level(run // 2 + 8, 4, True, metas[1], now, params[1], weights[1])
        run = run // 4

    blocks = now.reshape(2, 2, 4, HALF // 4).transpose(2, 0, 1, 3)
    blocks = jnp.broadcast_to(
        blocks[None, :, None], (2, 4, 2, 2, 2, HALF // 4)
    ).reshape(32, 2, HALF // 4)
    got = lax.all_to_all(blocks, ("zh", "co", "x"), 0, 0, tiled=True)
    got = got.reshape(2, 2, 2, 4, 2, HALF // 4)[:, :, :, 3]
    got = lax.dynamic_index_in_dim(got, x // 2, 1, keepdims=False)
    return lax.dynamic_index_in_dim(got, zh // 2, 1, keepdims=False)


def solution(mesh):
    finer = Mesh(mesh.devices.reshape(4, 2, 4, 4, 4), SECTION + SEQ)
    in_specs = (
        P(None, SEQ),
        P(),
        P(SECTION, None),
        P(SECTION, None, None),
        P(SECTION, SEQ, None),
    )
    out_specs = P(None, SEQ, SECTION)
    return jax.shard_map(
        shards, mesh=finer, in_specs=in_specs, out_specs=out_specs, check_vma=False
    )
```

```python
import jax
import jax.numpy as jnp
from jax import lax
from jax.experimental import pallas as pl
from jax.experimental.pallas import tpu as pltpu
from jax.sharding import Mesh
from jax.sharding import PartitionSpec as P


SEQ = ("zl", "y", "x")
SECTION = ("zh", "co")
C = 1536
HALF = C // 2
TAPS = 5
RUN = 1024
EDGE = 12
BLOCK = 96
SHIFTS = (0, 1, -1, 2)


def up16(rows):
    return -(-rows // 16) * 16


def activate(load, par_ref, a_scr, rows, edge, first, last):
    def step(i, carry):
        start = pl.multiple_of(i * 16, 16)
        left, right = load(start)
        squares = jnp.sum(left * left, axis=-1, keepdims=True)
        squares = squares + jnp.sum(right * right, axis=-1, keepdims=True)
        scale = lax.rsqrt(squares * (1.0 / C) + 1e-06)
        index = start + lax.broadcasted_iota(jnp.int32, (16, 1), 0)
        low = jnp.where(first == 1, edge, 0)
        high = jnp.where(last == 1, rows - edge, rows)
        inside = (index >= low) & (index < high)
        for side, part in enumerate((left, right)):
            lanes = pl.ds(side * HALF, HALF)
            value = part * scale * par_ref[0:1, lanes]
            value = jax.nn.gelu(value, approximate=True).astype(jnp.bfloat16)
            a_scr[pl.ds(start + 8, 16), lanes] = jnp.where(inside, value.astype(jnp.float32), 0.0)
        return carry

    lax.fori_loop(0, up16(rows) // 16, step, 0)


def spread(par_ref, a_scr, d_ref, rows):
    width = 384
    for lane in range(0, C, width):
        taps = [par_ref[1 + k : 2 + k, lane : lane + width] for k in range(TAPS)]

        def step(i, carry):
            start = pl.multiple_of(i * 16, 16)
            window = a_scr[pl.ds(start, 32), lane : lane + width]
            total = taps[0] * window[4:20]
            for k in range(1, TAPS):
                total = total + taps[k] * window[4 + 2 * k : 20 + 2 * k]
            d_ref[pl.ds(start, 16), lane : lane + width] = total.astype(jnp.bfloat16)
            return carry

        lax.fori_loop(0, up16(rows) // 16, step, 0)


def weight_copies(meta_ref, pieces, w_scr, sems):
    copies = []
    for p, piece in enumerate(pieces):
        for k in range(4):
            row = pl.multiple_of(meta_ref[3 + 4 * p + k] * BLOCK, 16)
            target = w_scr.at[pl.ds(row, BLOCK)]
            copies.append(pltpu.make_async_copy(piece.at[k], target, sems.at[4 * p + k]))
    return copies


def mix_and_pool(d_ref, w_scr, residual, y_scr, out_ref, rows, count):
    total = up16(rows)
    chunk = next(total // n for n in range(1, 99) if total % (16 * n) == 0 and total // n <= 272)
    for start in range(0, total, chunk):
        product = jnp.dot(
            d_ref[start : start + chunk], w_scr[...], preferred_element_type=jnp.float32
        )
        mixed = residual(start, chunk) + product
        for n in range(HALF // 128):
            y_scr[n, start : start + chunk] = mixed[:, 128 * n : 128 * n + 128]
    part = next(p for p in (128, 104, 64, 40, 16, 8, 4) if count % p == 0)
    for start in range(0, count, part):
        for n in range(HALF // 128):
            even = y_scr[n, pl.ds(4 + 2 * start, part, stride=2)]
            odd = y_scr[n, pl.ds(5 + 2 * start, part, stride=2)]
            pooled = jnp.maximum(even, odd).astype(jnp.bfloat16)
            out_ref[start : start + part, 128 * n : 128 * n + 128] = pooled


def first_half(rows, meta_ref, hot_ref, stem_ref, par_ref, x_ref, d_ref, x_scr, a_scr):
    chunk = 176
    for start in range(0, up16(rows), chunk):
        for side in range(2):
            x_scr[side, start : start + chunk] = jnp.dot(
                hot_ref[start : start + chunk],
                stem_ref[:, side * HALF : (side + 1) * HALF],
                preferred_element_type=jnp.float32,
            ).astype(jnp.bfloat16)

    def load(start):
        return [x_scr[side, pl.ds(start, 16)].astype(jnp.float32) for side in range(2)]

    activate(load, par_ref, a_scr, rows, EDGE, meta_ref[1], meta_ref[2])
    spread(par_ref, a_scr, d_ref, rows)
    x_ref[...] = x_scr[meta_ref[0]]


def second_half(rows, meta_ref, x_ref, d_ref, w0, w1, w2, w3, out_ref, w_scr, y_scr, sems):
    copies = weight_copies(meta_ref, (w0, w1, w2, w3), w_scr, sems)
    for copy in copies:
        copy.start()
    for copy in copies:
        copy.wait()

    def residual(start, chunk):
        return x_ref[start : start + chunk].astype(jnp.float32)

    mix_and_pool(d_ref, w_scr, residual, y_scr, out_ref, rows, (rows - 8) // 2)


def whole_level(
    rows, edge, meta_ref, x_refs, par_ref, w0, w1, w2, w3, out_ref, a_scr, d_scr, w_scr, y_scr, sems
):
    two = len(x_refs) == 2
    copies = weight_copies(meta_ref, (w0, w1, w2, w3), w_scr, sems)
    for copy in copies:
        copy.start()

    def load(start):
        if two:
            return [ref[pl.ds(start, 16)].astype(jnp.float32) for ref in x_refs]
        return [x_refs[0][side, pl.ds(start, 16)].astype(jnp.float32) for side in range(2)]

    activate(load, par_ref, a_scr, rows, edge, meta_ref[1], meta_ref[2])
    spread(par_ref, a_scr, d_scr, rows)
    for copy in copies:
        copy.wait()

    def residual(start, chunk):
        if two:
            return x_refs[0][start : start + chunk].astype(jnp.float32)
        return x_refs[0][meta_ref[0], start : start + chunk].astype(jnp.float32)

    mix_and_pool(d_scr, w_scr, residual, y_scr, out_ref, rows, (rows - 8) // 2)


def spec(memory_space=pltpu.VMEM):
    return pl.BlockSpec(memory_space=memory_space)


def out_rows(rows, last):
    return (rows - 8) // 2 if last else up16((rows - 8) // 2)


def run_first_half(rows, meta, hot, stem, par):
    size = up16(rows)
    return pl.pallas_call(
        lambda *refs: first_half(rows, *refs),
        in_specs=[spec(pltpu.SMEM), spec(), spec(), spec()],
        out_specs=[spec(), spec()],
        out_shape=[
            jax.ShapeDtypeStruct((size, HALF), jnp.bfloat16),
            jax.ShapeDtypeStruct((size, C), jnp.bfloat16),
        ],
        scratch_shapes=[
            pltpu.VMEM((2, size, HALF), jnp.bfloat16),
            pltpu.VMEM((size + 16, C), jnp.float32),
        ],
        name="stem_and_taps",
    )(meta, hot, stem, par)


def run_second_half(rows, meta, x, d, pieces):
    size = up16(rows)
    return pl.pallas_call(
        lambda *refs: second_half(rows, *refs),
        in_specs=[spec(pltpu.SMEM), spec(), spec()] + [spec(pl.ANY)] * 4,
        out_specs=spec(),
        out_shape=jax.ShapeDtypeStruct((out_rows(rows, False), HALF), jnp.bfloat16),
        scratch_shapes=[
            pltpu.VMEM((C, HALF), jnp.bfloat16),
            pltpu.VMEM((HALF // 128, size, 128), jnp.float32),
            pltpu.SemaphoreType.DMA((16,)),
        ],
        name="mix_first",
    )(meta, x, d, *pieces)


def run_level(rows, edge, last, meta, x, par, pieces):
    size = up16(rows)
    n = len(x)
    return pl.pallas_call(
        lambda meta_ref, *refs: whole_level(rows, edge, meta_ref, refs[:n], *refs[n:]),
        in_specs=[spec(pltpu.SMEM)] + [spec()] * (n + 1) + [spec(pl.ANY)] * 4,
        out_specs=spec(),
        out_shape=jax.ShapeDtypeStruct((out_rows(rows, last), HALF), jnp.bfloat16),
        scratch_shapes=[
            pltpu.VMEM((size + 16, C), jnp.float32),
            pltpu.VMEM((size, C), jnp.bfloat16),
            pltpu.VMEM((C, HALF), jnp.bfloat16),
            pltpu.VMEM((HALF // 128, size, 128), jnp.float32),
            pltpu.SemaphoreType.DMA((16,)),
        ],
    )(meta, *x, par, *pieces)


def ring(size, by):
    return [(i, (i + by) % size) for i in range(size)]


def around(array, axes, size):
    out = [array]
    for by in SHIFTS[1:]:
        out.append(lax.ppermute(array, axes, ring(size, by)))
    return out


def by_role(array, j):
    pairs = [
        (zs * 4 + x0, ((x0 - j) % 4) * 4 + zs) for zs in range(4) for x0 in range(4)
    ]
    return lax.ppermute(array, ("zh", "x"), pairs)


def flat(b, g, role):
    zh, zl, y = 2 * b + g % 2, g // 8, (g // 2) % 4
    return ((zh * 4 + zl) * 4 + y) * 4 + role


def gathered_bases(bases, sequence, before, count):
    mine = lax.dynamic_index_in_dim(bases + 1, sequence, 0, keepdims=False)
    parts = []
    for by in (-1, 0, 1, 2):
        pairs = []
        for zh in range(4):
            for row in range(16):
                place = 4 * row + 2 * (zh % 2) + by
                if 0 <= place < 64:
                    pairs.append((zh * 64 + place, zh * 64 + row * 4))
        parts.append(lax.ppermute(mine, ("zh", "zl", "y", "x"), pairs))
    return jnp.concatenate(parts)[mine.shape[0] - before :][:count]


def pass_on(array, role):
    rows = array.shape[0]
    axes = ("zh", "zl", "y", "x")
    up = [(flat(b, g, role), flat(b, g + 1, role + 1)) for b in range(2) for g in range(31)]
    down = [(flat(b, g + 1, role), flat(b, g, role + 1)) for b in range(2) for g in range(31)]
    before = lax.ppermute(array[rows - EDGE :], axes, up)
    after = lax.ppermute(array[:EDGE], axes, down)
    own = lax.ppermute(array, "x", [(role, role + 1)])
    blank = jnp.zeros((8, HALF), array.dtype)
    return jnp.concatenate([before, own, after, blank], axis=0)


def relay(bases, stem_weight, gains, depth_taps, point_weight):
    zh, co, zl, y, x = [lax.axis_index(name) for name in ("zh", "co", "zl", "y", "x")]
    margin = stem_weight.shape[0] // 2
    group = (zl * 4 + y) * 2 + zh % 2
    sequence = zh // 2

    params = jnp.concatenate(
        [gains, depth_taps[0], jnp.zeros((2, C), gains.dtype)], axis=0
    )
    params = by_role(lax.all_gather(params, "co"), 0).astype(jnp.float32)
    own = point_weight[0].reshape(-1, 2, HALF).transpose(1, 0, 2)
    own = lax.all_to_all(own, "co", 0, 0, tiled=True)
    turned = jnp.stack([by_role(own, j) for j in range(4)] * 2, axis=0)
    ordered = lax.dynamic_slice_in_dim(turned, (4 - zh) % 4, 4, 0)
    blocks = [ordered[:, slot].reshape(BLOCK, HALF) for slot in range(2)]
    along_z = around(blocks[0], ("zh", "zl"), 16)
    along_y = around(blocks[1], "y", 4)
    along_z, along_y = lax.optimization_barrier((jnp.stack(along_z), jnp.stack(along_y)))
    weights = [around(along_z, "y", 4), around(along_y, ("zh", "zl"), 16)]
    shift = jnp.array(SHIFTS, jnp.int32)
    z_of, y_of = (zl - shift) % 4, (y - shift) % 4
    places = [
        (z_of[None, :] * 4 + y_of[:, None]).reshape(-1),
        (z_of[:, None] * 4 + y_of[None, :]).reshape(-1),
    ]
    flags = jnp.stack([co, (group == 0).astype(jnp.int32), (group == 31).astype(jnp.int32)])
    metas = [jnp.concatenate([flags.astype(jnp.int32), place]) for place in places]
    own_first = jnp.concatenate([flags.astype(jnp.int32), (places[1] + 8 * co) % 16])
    swapped = jnp.concatenate([params[1][:, HALF:], params[1][:, :HALF]], axis=1)
    swapped = jnp.where(co == 0, params[1], swapped)

    rows = RUN + 2 * EDGE
    size = up16(rows)
    ids = gathered_bases(bases, sequence, EDGE + margin, size + 2 * margin)
    hot = (ids[:, None] == jnp.arange(1, 5, dtype=jnp.int32)[None, :]).astype(jnp.bfloat16)
    windows = [hot[k : k + size] for k in range(2 * margin + 1)]
    windows = jnp.concatenate(windows + [jnp.zeros((size, 4), jnp.bfloat16)], axis=1)
    stem = jnp.pad(stem_weight.reshape(-1, C), ((0, 4), (0, 0)))
    level_rows, taps = run_first_half(rows, metas[0], windows, stem, params[0])
    now = run_second_half(rows, metas[0], level_rows, taps, weights[0])
    other = lax.ppermute(now, "co", [(0, 1), (1, 0)])
    now = run_level(RUN // 2 + 8, 4, True, own_first, [now, other], swapped, weights[1])
    run = RUN // 4
    for role in range(3):
        now = lax.all_gather(pass_on(now, role), "co")
        now = run_level(run + 2 * EDGE, EDGE, False, metas[0], [now], params[0], weights[0])
        now = lax.all_gather(now, "co")
        now = run_level(run // 2 + 8, 4, True, metas[1], [now], params[1], weights[1])
        run = run // 4

    blocks = now.reshape(2, 2, 4, HALF // 4).transpose(2, 0, 1, 3)
    blocks = jnp.broadcast_to(
        blocks[None, :, None], (2, 4, 2, 2, 2, HALF // 4)
    ).reshape(32, 2, HALF // 4)
    got = lax.all_to_all(blocks, ("zh", "co", "x"), 0, 0, tiled=True)
    got = got.reshape(2, 2, 2, 4, 2, HALF // 4)[:, :, :, 3]
    got = lax.dynamic_index_in_dim(got, x // 2, 1, keepdims=False)
    return lax.dynamic_index_in_dim(got, zh // 2, 1, keepdims=False)


def solution(mesh):
    finer = Mesh(mesh.devices.reshape(4, 2, 4, 4, 4), SECTION + SEQ)
    in_specs = (
        P(None, SEQ),
        P(),
        P(SECTION, None),
        P(SECTION, None, None),
        P(SECTION, SEQ, None),
    )
    out_specs = P(None, SEQ, SECTION)
    return jax.shard_map(relay, mesh=finer, in_specs=in_specs, out_specs=out_specs, check_vma=False)
```

```python
import jax
import jax.numpy as jnp
from jax import lax
from jax.experimental import pallas as pl
from jax.experimental.pallas import tpu as pltpu
from jax.sharding import Mesh
from jax.sharding import PartitionSpec as P


SEQ = ("zl", "y", "x")
SECTION = ("zh", "co")
C = 1536
HALF = C // 2
TAPS = 5
RUN = 1024
EDGE = 12
BLOCK = 96
SHIFTS = (0, 1, -1, 2)
TILES = HALF // 128
GELU = 0.7978845608028654


def up16(rows):
    return -(-rows // 16) * 16


def even_chunk(rows, most):
    total = up16(rows)
    return next(total // n for n in range(1, 99) if total % (16 * n) == 0 and total // n <= most)


def activate(load, par_ref, a_scr, rows, edge, meta_ref):
    def step(i, carry):
        start = pl.multiple_of(i * 16, 16)
        parts = load(start)
        squares = jnp.sum(parts[0] * parts[0] + parts[1] * parts[1], axis=-1, keepdims=True)
        scale = lax.rsqrt(squares * (1.0 / C) + 1e-06)
        for side, part in enumerate(parts):
            value = part * scale * par_ref[0:1, side * HALF : (side + 1) * HALF]
            bent = jnp.tanh(value * (GELU + (GELU * 0.044715) * (value * value)))
            half = 0.5 * value
            value = (half + half * bent).astype(jnp.bfloat16).astype(jnp.float32)
            for t in range(TILES):
                tile = value[:, 128 * t : 128 * t + 128]
                a_scr[side * TILES + t, pl.ds(start + 8, 16)] = tile
        return carry

    lax.fori_loop(0, up16(rows) // 16, step, 0)

    @pl.when(meta_ref[1] == 1)
    def _():
        for t in range(2 * TILES):
            a_scr[t, 8 : 8 + edge] = jnp.zeros((edge, 128), jnp.float32)

    @pl.when(meta_ref[2] == 1)
    def _():
        for t in range(2 * TILES):
            a_scr[t, 8 + rows - edge : 8 + rows] = jnp.zeros((edge, 128), jnp.float32)


def spread(par_ref, a_scr, d_ref, rows):
    chunk = even_chunk(rows, 176)
    for t in range(2 * TILES):
        lanes = slice(128 * t, 128 * t + 128)
        taps = [par_ref[1 + k : 2 + k, lanes] for k in range(TAPS)]

        def step(i, carry):
            start = pl.multiple_of(i * chunk, 16)
            total = taps[0] * a_scr[t, pl.ds(start + 4, chunk)]
            for k in range(1, TAPS):
                total = total + taps[k] * a_scr[t, pl.ds(start + 4 + 2 * k, chunk)]
            d_ref[pl.ds(start, chunk), lanes] = total.astype(jnp.bfloat16)
            return carry

        lax.fori_loop(0, up16(rows) // chunk, step, 0)


def weight_copies(meta_ref, pieces, w_ref, sems):
    copies = []
    for piece in pieces:
        for k in range(piece.shape[0]):
            n = len(copies)
            row = pl.multiple_of(meta_ref[3 + n] * BLOCK, 16)
            copies.append(
                pltpu.make_async_copy(piece.at[k], w_ref.at[pl.ds(row, BLOCK)], sems.at[n])
            )
    return copies


def mix_and_pool(d_ref, w_ref, residual, y_scr, out_ref, rows):
    count = (rows - 8) // 2
    total = up16(rows)
    chunk = even_chunk(rows, 272)
    for start in range(0, total, chunk):
        product = jnp.dot(
            d_ref[start : start + chunk], w_ref[...], preferred_element_type=jnp.float32
        )
        mixed = residual(start, chunk) + product
        for n in range(TILES):
            y_scr[n, start : start + chunk] = mixed[:, 128 * n : 128 * n + 128]
    part = next(p for p in (128, 104, 64, 40, 16, 8, 4) if count % p == 0)
    for start in range(0, count, part):
        for n in range(TILES):
            even = y_scr[n, pl.ds(4 + 2 * start, part, stride=2)]
            odd = y_scr[n, pl.ds(5 + 2 * start, part, stride=2)]
            pooled = jnp.maximum(even, odd).astype(jnp.bfloat16)
            out_ref[start : start + part, 128 * n : 128 * n + 128] = pooled


def first_half(rows, meta_ref, hot_ref, stem_ref, par_ref, x_ref, d_ref, x_scr, a_scr):
    chunk = 176
    for start in range(0, up16(rows), chunk):
        for side, target in enumerate((x_ref, x_scr)):
            target[start : start + chunk] = jnp.dot(
                hot_ref[start : start + chunk],
                stem_ref[:, side * HALF : (side + 1) * HALF],
                preferred_element_type=jnp.float32,
            ).astype(jnp.bfloat16)

    def load(start):
        return [ref[pl.ds(start, 16)].astype(jnp.float32) for ref in (x_ref, x_scr)]

    activate(load, par_ref, a_scr, rows, EDGE, meta_ref)
    spread(par_ref, a_scr, d_ref, rows)


def second_half(rows, meta_ref, x_ref, d_ref, *refs):
    *pieces, out_ref, w_ref, y_scr, sems = refs
    copies = weight_copies(meta_ref, pieces, w_ref, sems)
    for copy in copies:
        copy.start()
    for copy in copies:
        copy.wait()

    def residual(start, chunk):
        return x_ref[start : start + chunk].astype(jnp.float32)

    mix_and_pool(d_ref, w_ref, residual, y_scr, out_ref, rows)


def swapped_level(rows, edge, meta_ref, own_ref, other_ref, par_ref, *refs):
    *pieces, out_ref, w_ref, a_scr, d_scr, y_scr, sems = refs
    copies = weight_copies(meta_ref, pieces, w_ref, sems)
    for copy in copies:
        copy.start()

    def load(start):
        return [ref[pl.ds(start, 16)].astype(jnp.float32) for ref in (own_ref, other_ref)]

    activate(load, par_ref, a_scr, rows, edge, meta_ref)
    spread(par_ref, a_scr, d_scr, rows)
    for copy in copies:
        copy.wait()

    def residual(start, chunk):
        return own_ref[start : start + chunk].astype(jnp.float32)

    mix_and_pool(d_scr, w_ref, residual, y_scr, out_ref, rows)


def paired_level(rows, edge, meta_ref, x_ref, par_ref, w_ref, out_ref, a_scr, d_scr, y_scr):
    own = meta_ref[0]

    def load(start):
        return [x_ref[side, pl.ds(start, 16)].astype(jnp.float32) for side in (own, 1 - own)]

    activate(load, par_ref, a_scr, rows, edge, meta_ref)
    spread(par_ref, a_scr, d_scr, rows)

    def residual(start, chunk):
        return x_ref[own, start : start + chunk].astype(jnp.float32)

    mix_and_pool(d_scr, w_ref, residual, y_scr, out_ref, rows)


def spec(memory_space=pltpu.VMEM):
    return pl.BlockSpec(memory_space=memory_space)


def out_rows(rows, last):
    return (rows - 8) // 2 if last else up16((rows - 8) // 2)


def scratch(rows, names):
    size = up16(rows)
    shapes = {
        "a": pltpu.VMEM((2 * TILES, size + 16, 128), jnp.float32),
        "d": pltpu.VMEM((size, C), jnp.bfloat16),
        "x": pltpu.VMEM((size, HALF), jnp.bfloat16),
        "y": pltpu.VMEM((TILES, size, 128), jnp.float32),
        "s": pltpu.SemaphoreType.DMA((16,)),
    }
    return [shapes[name] for name in names]


def half_rows(size, width=HALF):
    return jax.ShapeDtypeStruct((size, width), jnp.bfloat16)


def run_first_half(rows, meta, hot, stem, par):
    size = up16(rows)
    return pl.pallas_call(
        lambda *refs: first_half(rows, *refs),
        in_specs=[spec(pltpu.SMEM), spec(), spec(), spec()],
        out_specs=[spec(), spec()],
        out_shape=[half_rows(size), half_rows(size, C)],
        scratch_shapes=scratch(rows, "xa"),
        name="stem_and_taps",
    )(meta, hot, stem, par)


def run_second_half(rows, meta, x, d, pieces):
    return pl.pallas_call(
        lambda *refs: second_half(rows, *refs),
        in_specs=[spec(pltpu.SMEM), spec(), spec()] + [spec(pl.ANY)] * len(pieces),
        out_specs=[spec(), spec()],
        out_shape=[half_rows(out_rows(rows, False)), half_rows(C)],
        scratch_shapes=scratch(rows, "ys"),
        name="mix_first",
    )(meta, x, d, *pieces)


def run_swapped_level(rows, edge, meta, own, other, par, pieces):
    return pl.pallas_call(
        lambda *refs: swapped_level(rows, edge, *refs),
        in_specs=[spec(pltpu.SMEM)] + [spec()] * 3 + [spec(pl.ANY)] * len(pieces),
        out_specs=[spec(), spec()],
        out_shape=[half_rows(out_rows(rows, True)), half_rows(C)],
        scratch_shapes=scratch(rows, "adys"),
    )(meta, own, other, par, *pieces)


def run_level(rows, edge, last, meta, x, par, weights):
    return pl.pallas_call(
        lambda *refs: paired_level(rows, edge, *refs),
        in_specs=[spec(pltpu.SMEM)] + [spec()] * 3,
        out_specs=spec(),
        out_shape=half_rows(out_rows(rows, last)),
        scratch_shapes=scratch(rows, "ady"),
    )(meta, x, par, weights)


def ring(size, by):
    return [(i, (i + by) % size) for i in range(size)]


def around(array, axes, size):
    out = [array]
    for by in SHIFTS[1:]:
        out.append(lax.ppermute(array, axes, ring(size, by)))
    return out


def around_y(array):
    copies = lax.optimization_barrier(jnp.broadcast_to(array[None], (4, *array.shape)))
    return lax.all_to_all(copies, "y", 0, 0, tiled=True)


def own_first(array, co):
    turned = jnp.concatenate([array[..., HALF:], array[..., :HALF]], axis=-1)
    return jnp.where(co == 0, array, turned)


def flat(b, g, role):
    zh, zl, y = 2 * b + g % 2, g // 8, (g // 2) % 4
    return ((zh * 4 + zl) * 4 + y) * 4 + role


def gathered_bases(bases, sequence, before, count):
    mine = lax.dynamic_index_in_dim(bases + 1, sequence, 0, keepdims=False)
    parts = []
    for by in (-1, 0, 1, 2):
        pairs = []
        for zh in range(4):
            for row in range(16):
                place = 4 * row + 2 * (zh % 2) + by
                if 0 <= place < 64:
                    pairs.append((zh * 64 + place, zh * 64 + row * 4))
        parts.append(lax.ppermute(mine, ("zh", "zl", "y", "x"), pairs))
    return jnp.concatenate(parts)[mine.shape[0] - before :][:count]


def pass_on(array, role):
    rows = array.shape[0]
    axes = ("zh", "zl", "y", "x")
    up = [(flat(b, g, role), flat(b, g + 1, role + 1)) for b in range(2) for g in range(31)]
    down = [(flat(b, g + 1, role), flat(b, g, role + 1)) for b in range(2) for g in range(31)]
    before = lax.ppermute(array[rows - EDGE :], axes, up)
    after = lax.ppermute(array[:EDGE], axes, down)
    own = lax.ppermute(array, "x", [(role, role + 1)])
    blank = jnp.zeros((8, HALF), array.dtype)
    return jnp.concatenate([before, own, after, blank], axis=0)


def relay(bases, stem_weight, gains, depth_taps, point_weight):
    zh, co, zl, y, x = [lax.axis_index(name) for name in ("zh", "co", "zl", "y", "x")]
    margin = stem_weight.shape[0] // 2
    group = (zl * 4 + y) * 2 + zh % 2
    sequence = zh // 2

    held = [point_weight[0], gains, depth_taps[0], jnp.zeros((2, C), gains.dtype)]
    held = jnp.concatenate(held, axis=0).reshape(-1, 2, HALF).transpose(1, 0, 2)
    held = lax.all_to_all(held, "co", 0, 0, tiled=True)
    held = lax.all_to_all(lax.all_gather(held, "zh"), "x", 0, 0, tiled=True)
    params = lax.all_gather(held[0, :, 24:], "co").transpose(1, 2, 0, 3).reshape(2, 8, C)
    params = own_first(params, co).astype(jnp.float32)
    blocks = [held[:, slot, :24].reshape(BLOCK, HALF) for slot in range(2)]
    along_z = jnp.stack(around(blocks[0], ("zh", "zl"), 16))
    along_y = around_y(blocks[1])
    along_z, along_y = lax.optimization_barrier((along_z, along_y))
    pieces = [[around_y(along_z).reshape(16, BLOCK, HALF)], around(along_y, ("zh", "zl"), 16)]
    z_of = (zl - jnp.array(SHIFTS, jnp.int32)) % 4
    y_of = jnp.arange(4, dtype=jnp.int32)
    places = [z_of[None, :] * 4 + y_of[:, None], z_of[:, None] * 4 + y_of[None, :]]
    flags = jnp.stack([co, (group == 0).astype(jnp.int32), (group == 31).astype(jnp.int32)])
    metas = [
        jnp.concatenate([flags.astype(jnp.int32), (place.reshape(-1) + 8 * co) % 16])
        for place in places
    ]

    rows = RUN + 2 * EDGE
    size = up16(rows)
    ids = gathered_bases(bases, sequence, EDGE + margin, size + 2 * margin)
    windows = jnp.stack([ids[k : k + size] for k in range(2 * margin + 1)])
    kinds = jnp.arange(1, 5, dtype=jnp.int32)[None, :, None]
    hot = (windows[:, None, :] == kinds).astype(jnp.bfloat16).reshape(-1, size)
    hot = jnp.pad(hot, ((0, 4), (0, 0))).T
    stem = own_first(jnp.pad(stem_weight.reshape(-1, C), ((0, 4), (0, 0))), co)
    level_rows, taps = run_first_half(rows, metas[0], hot, stem, params[0])
    now, even_weights = run_second_half(rows, metas[0], level_rows, taps, pieces[0])
    other = lax.ppermute(now, "co", [(0, 1), (1, 0)])
    now, odd_weights = run_swapped_level(
        RUN // 2 + 8, 4, metas[1], now, other, params[1], pieces[1]
    )
    run = RUN // 4
    for role in range(3):
        now = lax.all_gather(pass_on(now, role), "co")
        now = run_level(run + 2 * EDGE, EDGE, False, metas[0], now, params[0], even_weights)
        now = lax.all_gather(now, "co")
        now = run_level(run // 2 + 8, 4, True, metas[1], now, params[1], odd_weights)
        run = run // 4

    blocks = now.reshape(2, 2, 4, HALF // 4).transpose(2, 0, 1, 3)
    blocks = jnp.broadcast_to(
        blocks[None, :, None], (2, 4, 2, 2, 2, HALF // 4)
    ).reshape(32, 2, HALF // 4)
    got = lax.all_to_all(blocks, ("zh", "co", "x"), 0, 0, tiled=True)
    got = got.reshape(2, 2, 2, 4, 2, HALF // 4)[:, :, :, 3]
    got = lax.dynamic_index_in_dim(got, x // 2, 1, keepdims=False)
    return lax.dynamic_index_in_dim(got, zh // 2, 1, keepdims=False)


def solution(mesh):
    finer = Mesh(mesh.devices.reshape(4, 2, 4, 4, 4), SECTION + SEQ)
    in_specs = (
        P(None, SEQ),
        P(),
        P(SECTION, None),
        P(SECTION, None, None),
        P(SECTION, SEQ, None),
    )
    out_specs = P(None, SEQ, SECTION)
    return jax.shard_map(relay, mesh=finer, in_specs=in_specs, out_specs=out_specs, check_vma=False)
```

```python
import jax
import jax.numpy as jnp
from jax import lax
from jax.experimental import pallas as pl
from jax.experimental.pallas import tpu as pltpu
from jax.sharding import Mesh
from jax.sharding import PartitionSpec as P


SEQ = ("zl", "y", "x")
SECTION = ("zh", "co")
C = 1536
HALF = C // 2
TAPS = 5
RUN = 1024
EDGE = 12
BLOCK = 96
SHIFTS = (0, 1, -1, 2)
TILES = HALF // 128
GELU = 0.7978845608028654


def up16(rows):
    return -(-rows // 16) * 16


def even_chunk(rows, most):
    total = up16(rows)
    return next(total // n for n in range(1, 99) if total % (16 * n) == 0 and total // n <= most)


def activate(load, par_ref, a_scr, rows, edge, meta_ref):
    def step(i, carry):
        start = pl.multiple_of(i * 16, 16)
        parts = load(start)
        squares = jnp.sum(parts[0] * parts[0] + parts[1] * parts[1], axis=-1, keepdims=True)
        scale = lax.rsqrt(squares * (1.0 / C) + 1e-06)
        for side, part in enumerate(parts):
            value = part * scale * par_ref[0:1, side * HALF : (side + 1) * HALF]
            bent = jnp.tanh(value * (GELU + (GELU * 0.044715) * (value * value)))
            half = 0.5 * value
            value = (half + half * bent).astype(jnp.bfloat16).astype(jnp.float32)
            for t in range(TILES):
                tile = value[:, 128 * t : 128 * t + 128]
                a_scr[side * TILES + t, pl.ds(start + 8, 16)] = tile
        return carry

    lax.fori_loop(0, up16(rows) // 16, step, 0)

    @pl.when(meta_ref[1] == 1)
    def _():
        for t in range(2 * TILES):
            a_scr[t, 8 : 8 + edge] = jnp.zeros((edge, 128), jnp.float32)

    @pl.when(meta_ref[2] == 1)
    def _():
        for t in range(2 * TILES):
            a_scr[t, 8 + rows - edge : 8 + rows] = jnp.zeros((edge, 128), jnp.float32)


def spread(par_ref, a_scr, d_ref, rows):
    chunk = even_chunk(rows, 176)
    for t in range(2 * TILES):
        lanes = slice(128 * t, 128 * t + 128)
        taps = [par_ref[1 + k : 2 + k, lanes] for k in range(TAPS)]

        def step(i, carry):
            start = pl.multiple_of(i * chunk, 16)
            total = taps[0] * a_scr[t, pl.ds(start + 4, chunk)]
            for k in range(1, TAPS):
                total = total + taps[k] * a_scr[t, pl.ds(start + 4 + 2 * k, chunk)]
            d_ref[pl.ds(start, chunk), lanes] = total.astype(jnp.bfloat16)
            return carry

        lax.fori_loop(0, up16(rows) // chunk, step, 0)


def weight_copies(meta_ref, pieces, w_ref, sems):
    copies = []
    for piece in pieces:
        for k in range(piece.shape[0]):
            n = len(copies)
            row = pl.multiple_of(meta_ref[3 + n] * BLOCK, 16)
            copies.append(
                pltpu.make_async_copy(piece.at[k], w_ref.at[pl.ds(row, BLOCK)], sems.at[n])
            )
    return copies


def mix_and_pool(d_ref, w_ref, residual, y_scr, out_ref, rows):
    count = (rows - 8) // 2
    total = up16(rows)
    chunk = even_chunk(rows, 272)
    for start in range(0, total, chunk):
        product = jnp.dot(
            d_ref[start : start + chunk], w_ref[...], preferred_element_type=jnp.float32
        )
        mixed = residual(start, chunk) + product
        for n in range(TILES):
            y_scr[n, start : start + chunk] = mixed[:, 128 * n : 128 * n + 128]
    part = next(p for p in (128, 104, 64, 40, 16, 8, 4) if count % p == 0)
    for start in range(0, count, part):
        for n in range(TILES):
            even = y_scr[n, pl.ds(4 + 2 * start, part, stride=2)]
            odd = y_scr[n, pl.ds(5 + 2 * start, part, stride=2)]
            pooled = jnp.maximum(even, odd).astype(jnp.bfloat16)
            out_ref[start : start + part, 128 * n : 128 * n + 128] = pooled


def first_half(rows, meta_ref, hot_ref, stem_ref, par_ref, x_ref, d_ref, x_scr, a_scr):
    chunk = 176
    for start in range(0, up16(rows), chunk):
        for side, target in enumerate((x_ref, x_scr)):
            target[start : start + chunk] = jnp.dot(
                hot_ref[start : start + chunk],
                stem_ref[:, side * HALF : (side + 1) * HALF],
                preferred_element_type=jnp.float32,
            ).astype(jnp.bfloat16)

    def load(start):
        return [ref[pl.ds(start, 16)].astype(jnp.float32) for ref in (x_ref, x_scr)]

    activate(load, par_ref, a_scr, rows, EDGE, meta_ref)
    spread(par_ref, a_scr, d_ref, rows)


def second_half(rows, meta_ref, x_ref, d_ref, *refs):
    *pieces, out_ref, w_ref, y_scr, sems = refs
    copies = weight_copies(meta_ref, pieces, w_ref, sems)
    for copy in copies:
        copy.start()
    for copy in copies:
        copy.wait()

    def residual(start, chunk):
        return x_ref[start : start + chunk].astype(jnp.float32)

    mix_and_pool(d_ref, w_ref, residual, y_scr, out_ref, rows)


def swapped_level(rows, edge, meta_ref, own_ref, other_ref, par_ref, *refs):
    *pieces, out_ref, w_ref, a_scr, d_scr, y_scr, sems = refs
    copies = weight_copies(meta_ref, pieces, w_ref, sems)
    for copy in copies:
        copy.start()

    def load(start):
        return [ref[pl.ds(start, 16)].astype(jnp.float32) for ref in (own_ref, other_ref)]

    activate(load, par_ref, a_scr, rows, edge, meta_ref)
    spread(par_ref, a_scr, d_scr, rows)
    for copy in copies:
        copy.wait()

    def residual(start, chunk):
        return own_ref[start : start + chunk].astype(jnp.float32)

    mix_and_pool(d_scr, w_ref, residual, y_scr, out_ref, rows)


def paired_level(rows, edge, meta_ref, x_ref, par_ref, w_ref, out_ref, a_scr, d_scr, y_scr):
    own = meta_ref[0]

    def load(start):
        return [x_ref[side, pl.ds(start, 16)].astype(jnp.float32) for side in (own, 1 - own)]

    activate(load, par_ref, a_scr, rows, edge, meta_ref)
    spread(par_ref, a_scr, d_scr, rows)

    def residual(start, chunk):
        return x_ref[own, start : start + chunk].astype(jnp.float32)

    mix_and_pool(d_scr, w_ref, residual, y_scr, out_ref, rows)


def spec(memory_space=pltpu.VMEM):
    return pl.BlockSpec(memory_space=memory_space)


def out_rows(rows, last):
    return (rows - 8) // 2 if last else up16((rows - 8) // 2)


def scratch(rows, names):
    size = up16(rows)
    shapes = {
        "a": pltpu.VMEM((2 * TILES, size + 16, 128), jnp.float32),
        "d": pltpu.VMEM((size, C), jnp.bfloat16),
        "x": pltpu.VMEM((size, HALF), jnp.bfloat16),
        "y": pltpu.VMEM((TILES, size, 128), jnp.float32),
        "s": pltpu.SemaphoreType.DMA((16,)),
    }
    return [shapes[name] for name in names]


def half_rows(size, width=HALF):
    return jax.ShapeDtypeStruct((size, width), jnp.bfloat16)


def run_first_half(rows, meta, hot, stem, par):
    size = up16(rows)
    return pl.pallas_call(
        lambda *refs: first_half(rows, *refs),
        in_specs=[spec(pltpu.SMEM), spec(), spec(), spec()],
        out_specs=[spec(), spec()],
        out_shape=[half_rows(size), half_rows(size, C)],
        scratch_shapes=scratch(rows, "xa"),
        name="stem_and_taps",
    )(meta, hot, stem, par)


def run_second_half(rows, meta, x, d, pieces):
    return pl.pallas_call(
        lambda *refs: second_half(rows, *refs),
        in_specs=[spec(pltpu.SMEM), spec(), spec()] + [spec()] * len(pieces),
        out_specs=[spec(), spec()],
        out_shape=[half_rows(out_rows(rows, False)), half_rows(C)],
        scratch_shapes=scratch(rows, "ys"),
        name="mix_first",
    )(meta, x, d, *pieces)


def run_swapped_level(rows, edge, meta, own, other, par, pieces):
    return pl.pallas_call(
        lambda *refs: swapped_level(rows, edge, *refs),
        in_specs=[spec(pltpu.SMEM)] + [spec()] * 3 + [spec()] * len(pieces),
        out_specs=[spec(), spec()],
        out_shape=[half_rows(out_rows(rows, True)), half_rows(C)],
        scratch_shapes=scratch(rows, "adys"),
    )(meta, own, other, par, *pieces)


def run_level(rows, edge, last, meta, x, par, weights):
    return pl.pallas_call(
        lambda *refs: paired_level(rows, edge, *refs),
        in_specs=[spec(pltpu.SMEM)] + [spec()] * 3,
        out_specs=spec(),
        out_shape=half_rows(out_rows(rows, last)),
        scratch_shapes=scratch(rows, "ady"),
    )(meta, x, par, weights)


def ring(size, by):
    return [(i, (i + by) % size) for i in range(size)]


def around_z(array):
    sends = [(array, 1), (array, -1), (array[:2], 2), (array[2:], -2)]
    out = [array]
    for part, by in sends:
        out.append(lax.ppermute(part, ("zh", "zl"), ring(16, by)))
    return out


def to_roles(array, axis):
    copies = jnp.broadcast_to(array[None], (4, *array.shape)).reshape(16, *array.shape[1:])
    copies = lax.optimization_barrier(copies)
    got = lax.all_to_all(copies, (axis, "x"), 0, 0, tiled=True)
    return got.reshape(4, BLOCK, HALF)


def around_y(array):
    copies = lax.optimization_barrier(jnp.broadcast_to(array[None], (4, *array.shape)))
    return lax.all_to_all(copies, "y", 0, 0, tiled=True)


def own_first(array, co):
    turned = jnp.concatenate([array[..., HALF:], array[..., :HALF]], axis=-1)
    return jnp.where(co == 0, array, turned)


def flat(b, g, role):
    zh, zl, y = 2 * b + g % 2, g // 8, (g // 2) % 4
    return ((zh * 4 + zl) * 4 + y) * 4 + role


def gathered_bases(bases, sequence, before, count):
    mine = lax.dynamic_index_in_dim(bases + 1, sequence, 0, keepdims=False)
    parts = []
    for by in (-1, 0, 1, 2):
        pairs = []
        for zh in range(4):
            for row in range(16):
                place = 4 * row + 2 * (zh % 2) + by
                if 0 <= place < 64:
                    pairs.append((zh * 64 + place, zh * 64 + row * 4))
        parts.append(lax.ppermute(mine, ("zh", "zl", "y", "x"), pairs))
    return jnp.concatenate(parts)[mine.shape[0] - before :][:count]


def pass_on(array, role):
    rows = array.shape[0]
    axes = ("zh", "zl", "y", "x")
    up = [(flat(b, g, role), flat(b, g + 1, role + 1)) for b in range(2) for g in range(31)]
    down = [(flat(b, g + 1, role), flat(b, g, role + 1)) for b in range(2) for g in range(31)]
    before = lax.ppermute(array[rows - EDGE :], axes, up)
    after = lax.ppermute(array[:EDGE], axes, down)
    own = lax.ppermute(array, "x", [(role, role + 1)])
    blank = jnp.zeros((8, HALF), array.dtype)
    return jnp.concatenate([before, own, after, blank], axis=0)


def relay(bases, stem_weight, gains, depth_taps, point_weight):
    zh, co, zl, y, x = [lax.axis_index(name) for name in ("zh", "co", "zl", "y", "x")]
    margin = stem_weight.shape[0] // 2
    group = (zl * 4 + y) * 2 + zh % 2
    sequence = zh // 2

    held = [point_weight[0], gains, depth_taps[0], jnp.zeros((2, C), gains.dtype)]
    held = jnp.concatenate(held, axis=0).reshape(-1, 2, HALF).transpose(1, 0, 2)
    held = lax.all_to_all(held, "co", 0, 0, tiled=True)
    held, bases = lax.optimization_barrier((lax.all_gather(held, "zh"), bases))
    along_z = to_roles(held[:, 0, :24], "zl")
    along_y = to_roles(held[:, 1, :24], "y")
    along_z, along_y = lax.optimization_barrier((along_z, along_y))
    pieces = [[around_y(along_z).reshape(16, BLOCK, HALF)], around_z(along_y)]
    params = lax.dynamic_index_in_dim(held, x, 0, keepdims=False)[:, 24:]
    params = lax.all_gather(params, "co")
    params = params.transpose(1, 2, 0, 3).reshape(2, 8, C)
    params = own_first(params, co).astype(jnp.float32)
    four = jnp.arange(4, dtype=jnp.int32)
    z_of = (zl - jnp.array(SHIFTS, jnp.int32)) % 4
    places = [four[None, :] * 4 + four[:, None], z_of[:, None] * 4 + four[None, :]]
    flags = jnp.stack([co, (group == 0).astype(jnp.int32), (group == 31).astype(jnp.int32)])
    metas = [
        jnp.concatenate([flags.astype(jnp.int32), (place.reshape(-1) + 8 * co) % 16])
        for place in places
    ]

    rows = RUN + 2 * EDGE
    size = up16(rows)
    ids = gathered_bases(bases, sequence, EDGE + margin, size + 2 * margin)
    windows = jnp.stack([ids[k : k + size] for k in range(2 * margin + 1)])
    kinds = jnp.arange(1, 5, dtype=jnp.int32)[None, :, None]
    hot = (windows[:, None, :] == kinds).astype(jnp.bfloat16).reshape(-1, size)
    hot = jnp.pad(hot, ((0, 4), (0, 0))).T
    stem = own_first(jnp.pad(stem_weight.reshape(-1, C), ((0, 4), (0, 0))), co)
    level_rows, taps = run_first_half(rows, metas[0], hot, stem, params[0])
    now, even_weights = run_second_half(rows, metas[0], level_rows, taps, pieces[0])
    other = lax.ppermute(now, "co", [(0, 1), (1, 0)])
    now, odd_weights = run_swapped_level(
        RUN // 2 + 8, 4, metas[1], now, other, params[1], pieces[1]
    )
    run = RUN // 4
    for role in range(3):
        now = lax.all_gather(pass_on(now, role), "co")
        now = run_level(run + 2 * EDGE, EDGE, False, metas[0], now, params[0], even_weights)
        now = lax.all_gather(now, "co")
        now = run_level(run // 2 + 8, 4, True, metas[1], now, params[1], odd_weights)
        run = run // 4

    blocks = now.reshape(2, 2, 4, HALF // 4).transpose(2, 0, 1, 3)
    blocks = jnp.broadcast_to(
        blocks[None, :, None], (2, 4, 2, 2, 2, HALF // 4)
    ).reshape(32, 2, HALF // 4)
    got = lax.all_to_all(blocks, ("zh", "co", "x"), 0, 0, tiled=True)
    got = got.reshape(2, 2, 2, 4, 2, HALF // 4)[:, :, :, 3]
    got = lax.dynamic_index_in_dim(got, x // 2, 1, keepdims=False)
    return lax.dynamic_index_in_dim(got, zh // 2, 1, keepdims=False)


def solution(mesh):
    finer = Mesh(mesh.devices.reshape(4, 2, 4, 4, 4), SECTION + SEQ)
    in_specs = (
        P(None, SEQ),
        P(),
        P(SECTION, None),
        P(SECTION, None, None),
        P(SECTION, SEQ, None),
    )
    out_specs = P(None, SEQ, SECTION)
    return jax.shard_map(relay, mesh=finer, in_specs=in_specs, out_specs=out_specs, check_vma=False)
```

```python
import jax
import jax.numpy as jnp
from jax import lax
from jax.experimental import pallas as pl
from jax.experimental.pallas import tpu as pltpu
from jax.sharding import Mesh
from jax.sharding import PartitionSpec as P


SEQ = ("zl", "y", "x")
SECTION = ("zh", "co")
C = 1536
HALF = C // 2
TAPS = 5
RUN = 1024
EDGE = 12
BLOCK = 96
SHIFTS = (0, 1, -1, 2)
TILES = HALF // 128
GELU = 0.7978845608028654


def up16(rows):
    return -(-rows // 16) * 16


def even_chunk(rows, most):
    total = up16(rows)
    return next(total // n for n in range(1, 99) if total % (16 * n) == 0 and total // n <= most)


def activate(load, par_ref, a_scr, rows, edge, meta_ref):
    def step(i, carry):
        start = pl.multiple_of(i * 16, 16)
        parts = load(start)
        squares = jnp.sum(parts[0] * parts[0] + parts[1] * parts[1], axis=-1, keepdims=True)
        scale = lax.rsqrt(squares * (1.0 / C) + 1e-06)
        for side, part in enumerate(parts):
            value = part * scale * par_ref[0:1, side * HALF : (side + 1) * HALF]
            bent = jnp.tanh(value * (GELU + (GELU * 0.044715) * (value * value)))
            half = 0.5 * value
            value = (half + half * bent).astype(jnp.bfloat16).astype(jnp.float32)
            for t in range(TILES):
                tile = value[:, 128 * t : 128 * t + 128]
                a_scr[side * TILES + t, pl.ds(start + 8, 16)] = tile
        return carry

    lax.fori_loop(0, up16(rows) // 16, step, 0)

    @pl.when(meta_ref[1] == 1)
    def _():
        for t in range(2 * TILES):
            a_scr[t, 8 : 8 + edge] = jnp.zeros((edge, 128), jnp.float32)

    @pl.when(meta_ref[2] == 1)
    def _():
        for t in range(2 * TILES):
            a_scr[t, 8 + rows - edge : 8 + rows] = jnp.zeros((edge, 128), jnp.float32)


def spread(par_ref, a_scr, d_ref, rows):
    chunk = even_chunk(rows, 176)
    for t in range(2 * TILES):
        lanes = slice(128 * t, 128 * t + 128)
        taps = [par_ref[1 + k : 2 + k, lanes] for k in range(TAPS)]

        def step(i, carry):
            start = pl.multiple_of(i * chunk, 16)
            total = taps[0] * a_scr[t, pl.ds(start + 4, chunk)]
            for k in range(1, TAPS):
                total = total + taps[k] * a_scr[t, pl.ds(start + 4 + 2 * k, chunk)]
            d_ref[pl.ds(start, chunk), lanes] = total.astype(jnp.bfloat16)
            return carry

        lax.fori_loop(0, up16(rows) // chunk, step, 0)


def weight_copies(slot, meta_ref, pieces, w_ref, sems):
    copies = []
    for piece in pieces:
        for k in range(4):
            n = len(copies)
            row = pl.multiple_of(meta_ref[3 + n] * BLOCK, 16)
            source = piece.at[k, slot] if len(piece.shape) == 4 else piece.at[k]
            copies.append(
                pltpu.make_async_copy(source, w_ref.at[pl.ds(row, BLOCK)], sems.at[n])
            )
    return copies


def mix_and_pool(d_ref, w_ref, residual, y_scr, out_ref, rows):
    count = (rows - 8) // 2
    total = up16(rows)
    chunk = even_chunk(rows, 272)
    for start in range(0, total, chunk):
        product = jnp.dot(
            d_ref[start : start + chunk], w_ref[...], preferred_element_type=jnp.float32
        )
        mixed = residual(start, chunk) + product
        for n in range(TILES):
            y_scr[n, start : start + chunk] = mixed[:, 128 * n : 128 * n + 128]
    part = next(p for p in (128, 104, 64, 40, 16, 8, 4) if count % p == 0)
    for start in range(0, count, part):
        for n in range(TILES):
            even = y_scr[n, pl.ds(4 + 2 * start, part, stride=2)]
            odd = y_scr[n, pl.ds(5 + 2 * start, part, stride=2)]
            pooled = jnp.maximum(even, odd).astype(jnp.bfloat16)
            out_ref[start : start + part, 128 * n : 128 * n + 128] = pooled


def first_half(rows, meta_ref, hot_ref, stem_ref, par_ref, x_ref, d_ref, x_scr, a_scr):
    chunk = 176
    for start in range(0, up16(rows), chunk):
        for side, target in enumerate((x_ref, x_scr)):
            target[start : start + chunk] = jnp.dot(
                hot_ref[start : start + chunk],
                stem_ref[:, side * HALF : (side + 1) * HALF],
                preferred_element_type=jnp.float32,
            ).astype(jnp.bfloat16)

    def load(start):
        return [ref[pl.ds(start, 16)].astype(jnp.float32) for ref in (x_ref, x_scr)]

    activate(load, par_ref, a_scr, rows, EDGE, meta_ref)
    spread(par_ref, a_scr, d_ref, rows)


def second_half(rows, meta_ref, x_ref, d_ref, *refs):
    *pieces, out_ref, w_ref, y_scr, sems = refs
    copies = weight_copies(0, meta_ref, pieces, w_ref, sems)
    for copy in copies:
        copy.start()
    for copy in copies:
        copy.wait()

    def residual(start, chunk):
        return x_ref[start : start + chunk].astype(jnp.float32)

    mix_and_pool(d_ref, w_ref, residual, y_scr, out_ref, rows)


def swapped_level(rows, edge, meta_ref, own_ref, other_ref, par_ref, *refs):
    *pieces, out_ref, w_ref, a_scr, d_scr, y_scr, sems = refs
    copies = weight_copies(1, meta_ref, pieces, w_ref, sems)
    for copy in copies:
        copy.start()

    def load(start):
        return [ref[pl.ds(start, 16)].astype(jnp.float32) for ref in (own_ref, other_ref)]

    activate(load, par_ref, a_scr, rows, edge, meta_ref)
    spread(par_ref, a_scr, d_scr, rows)
    for copy in copies:
        copy.wait()

    def residual(start, chunk):
        return own_ref[start : start + chunk].astype(jnp.float32)

    mix_and_pool(d_scr, w_ref, residual, y_scr, out_ref, rows)


def paired_level(rows, edge, meta_ref, x_ref, par_ref, w_ref, out_ref, a_scr, d_scr, y_scr):
    own = meta_ref[0]

    def load(start):
        return [x_ref[side, pl.ds(start, 16)].astype(jnp.float32) for side in (own, 1 - own)]

    activate(load, par_ref, a_scr, rows, edge, meta_ref)
    spread(par_ref, a_scr, d_scr, rows)

    def residual(start, chunk):
        return x_ref[own, start : start + chunk].astype(jnp.float32)

    mix_and_pool(d_scr, w_ref, residual, y_scr, out_ref, rows)


def spec(memory_space=pltpu.VMEM):
    return pl.BlockSpec(memory_space=memory_space)


def out_rows(rows, last):
    return (rows - 8) // 2 if last else up16((rows - 8) // 2)


def scratch(rows, names):
    size = up16(rows)
    shapes = {
        "a": pltpu.VMEM((2 * TILES, size + 16, 128), jnp.float32),
        "d": pltpu.VMEM((size, C), jnp.bfloat16),
        "x": pltpu.VMEM((size, HALF), jnp.bfloat16),
        "y": pltpu.VMEM((TILES, size, 128), jnp.float32),
        "s": pltpu.SemaphoreType.DMA((16,)),
    }
    return [shapes[name] for name in names]


def half_rows(size, width=HALF):
    return jax.ShapeDtypeStruct((size, width), jnp.bfloat16)


def run_first_half(rows, meta, hot, stem, par):
    size = up16(rows)
    return pl.pallas_call(
        lambda *refs: first_half(rows, *refs),
        in_specs=[spec(pltpu.SMEM), spec(), spec(), spec()],
        out_specs=[spec(), spec()],
        out_shape=[half_rows(size), half_rows(size, C)],
        scratch_shapes=scratch(rows, "xa"),
        name="stem_and_taps",
    )(meta, hot, stem, par)


def run_second_half(rows, meta, x, d, pieces):
    return pl.pallas_call(
        lambda *refs: second_half(rows, *refs),
        in_specs=[spec(pltpu.SMEM), spec(), spec()] + [spec(pl.ANY)] * len(pieces),
        out_specs=[spec(), spec()],
        out_shape=[half_rows(out_rows(rows, False)), half_rows(C)],
        scratch_shapes=scratch(rows, "ys"),
        name="mix_first",
    )(meta, x, d, *pieces)


def run_swapped_level(rows, edge, meta, own, other, par, pieces):
    return pl.pallas_call(
        lambda *refs: swapped_level(rows, edge, *refs),
        in_specs=[spec(pltpu.SMEM)] + [spec()] * 3 + [spec(pl.ANY)] * len(pieces),
        out_specs=[spec(), spec()],
        out_shape=[half_rows(out_rows(rows, True)), half_rows(C)],
        scratch_shapes=scratch(rows, "adys"),
    )(meta, own, other, par, *pieces)


def run_level(rows, edge, last, meta, x, par, weights):
    return pl.pallas_call(
        lambda *refs: paired_level(rows, edge, *refs),
        in_specs=[spec(pltpu.SMEM)] + [spec()] * 3,
        out_specs=spec(),
        out_shape=half_rows(out_rows(rows, last)),
        scratch_shapes=scratch(rows, "ady"),
    )(meta, x, par, weights)


def ring(size, by):
    return [(i, (i + by) % size) for i in range(size)]


def around_y(array):
    copies = lax.optimization_barrier(jnp.broadcast_to(array[None], (4, *array.shape)))
    return lax.all_to_all(copies, "y", 0, 0, tiled=True)


def own_first(array, co):
    turned = jnp.concatenate([array[..., HALF:], array[..., :HALF]], axis=-1)
    return jnp.where(co == 0, array, turned)


def flat(b, g, role):
    zh, zl, y = 2 * b + g % 2, g // 8, (g // 2) % 4
    return ((zh * 4 + zl) * 4 + y) * 4 + role


def gathered_bases(bases, sequence, before, count):
    mine = lax.dynamic_index_in_dim(bases + 1, sequence, 0, keepdims=False)
    parts = []
    for by in (-1, 0, 1, 2):
        pairs = []
        for zh in range(4):
            for row in range(16):
                place = 4 * row + 2 * (zh % 2) + by
                if 0 <= place < 64:
                    pairs.append((zh * 64 + place, zh * 64 + row * 4))
        parts.append(lax.ppermute(mine, ("zh", "zl", "y", "x"), pairs))
    return jnp.concatenate(parts)[mine.shape[0] - before :][:count]


def pass_on(array, role):
    rows = array.shape[0]
    axes = ("zh", "zl", "y", "x")
    up = [(flat(b, g, role), flat(b, g + 1, role + 1)) for b in range(2) for g in range(31)]
    down = [(flat(b, g + 1, role), flat(b, g, role + 1)) for b in range(2) for g in range(31)]
    before = lax.ppermute(array[rows - EDGE :], axes, up)
    after = lax.ppermute(array[:EDGE], axes, down)
    own = lax.ppermute(array, "x", [(role, role + 1)])
    blank = jnp.zeros((8, HALF), array.dtype)
    return jnp.concatenate([before, own, after, blank], axis=0)


def relay(bases, stem_weight, gains, depth_taps, point_weight):
    zh, co, zl, y, x = [lax.axis_index(name) for name in ("zh", "co", "zl", "y", "x")]
    margin = stem_weight.shape[0] // 2
    group = (zl * 4 + y) * 2 + zh % 2
    sequence = zh // 2

    held = [point_weight[0], gains, depth_taps[0], jnp.zeros((2, C), gains.dtype)]
    held = lax.all_gather(jnp.concatenate(held, axis=0), "zh")
    held, bases = lax.optimization_barrier((held, bases))
    blocks = held[:, :24].reshape(4, 24, 2, HALF).transpose(2, 0, 1, 3)
    blocks = jnp.broadcast_to(blocks[:, None], (2, 4, 4, 24, HALF)).reshape(32, 24, HALF)
    blocks = lax.optimization_barrier(blocks)
    blocks = lax.all_to_all(blocks, ("co", "y", "x"), 0, 0, tiled=True)
    near = lax.optimization_barrier(blocks.reshape(2, 4, BLOCK, HALF))
    share = lax.dynamic_index_in_dim(near, y, 1, keepdims=False)
    share0 = lax.ppermute(share[0], ("zh", "zl"), ring(16, 2))
    share1 = lax.ppermute(share[1], ("zh", "zl"), ring(16, -2))
    beside = []
    for slot in range(2):
        sides = [near[slot]]
        for by in (1, -1):
            sides.append(lax.ppermute(near[slot], ("zh", "zl"), ring(16, by)))
        beside.append(sides)
    opposite = around_y(jnp.stack([share0, share1]))
    pieces = [sides + [opposite] for sides in beside]
    params = lax.dynamic_index_in_dim(held, x, 0, keepdims=False)[24:]
    params = lax.all_gather(params, "co")
    params = own_first(params, co).astype(jnp.float32)
    four = jnp.arange(4, dtype=jnp.int32)
    z_of = (zl - jnp.array(SHIFTS, jnp.int32)) % 4
    place = (z_of[:, None] * 4 + four[None, :]).reshape(-1)
    flags = jnp.stack([co, (group == 0).astype(jnp.int32), (group == 31).astype(jnp.int32)])
    meta = jnp.concatenate([flags.astype(jnp.int32), (place + 8 * co) % 16])

    rows = RUN + 2 * EDGE
    size = up16(rows)
    ids = gathered_bases(bases, sequence, EDGE + margin, size + 2 * margin)
    windows = jnp.stack([ids[k : k + size] for k in range(2 * margin + 1)])
    kinds = jnp.arange(1, 5, dtype=jnp.int32)[None, :, None]
    hot = (windows[:, None, :] == kinds).astype(jnp.bfloat16).reshape(-1, size)
    hot = jnp.pad(hot, ((0, 4), (0, 0))).T
    stem = own_first(jnp.pad(stem_weight.reshape(-1, C), ((0, 4), (0, 0))), co)
    level_rows, taps = run_first_half(rows, meta, hot, stem, params[0])
    now, even_weights = run_second_half(rows, meta, level_rows, taps, pieces[0])
    other = lax.ppermute(now, "co", [(0, 1), (1, 0)])
    now, odd_weights = run_swapped_level(
        RUN // 2 + 8, 4, meta, now, other, params[1], pieces[1]
    )
    run = RUN // 4
    for role in range(3):
        now = lax.all_gather(pass_on(now, role), "co")
        now = run_level(run + 2 * EDGE, EDGE, False, meta, now, params[0], even_weights)
        now = lax.all_gather(now, "co")
        now = run_level(run // 2 + 8, 4, True, meta, now, params[1], odd_weights)
        run = run // 4

    blocks = now.reshape(2, 2, 4, HALF // 4).transpose(2, 0, 1, 3)
    blocks = jnp.broadcast_to(
        blocks[None, :, None], (2, 4, 2, 2, 2, HALF // 4)
    ).reshape(32, 2, HALF // 4)
    got = lax.all_to_all(blocks, ("zh", "co", "x"), 0, 0, tiled=True)
    got = got.reshape(2, 2, 2, 4, 2, HALF // 4)[:, :, :, 3]
    got = lax.dynamic_index_in_dim(got, x // 2, 1, keepdims=False)
    return lax.dynamic_index_in_dim(got, zh // 2, 1, keepdims=False)


def solution(mesh):
    finer = Mesh(mesh.devices.reshape(4, 2, 4, 4, 4), SECTION + SEQ)
    in_specs = (
        P(None, SEQ),
        P(),
        P(SECTION, None),
        P(SECTION, None, None),
        P(SECTION, SEQ, None),
    )
    out_specs = P(None, SEQ, SECTION)
    return jax.shard_map(relay, mesh=finer, in_specs=in_specs, out_specs=out_specs, check_vma=False)
```

```python
import jax
import jax.numpy as jnp
from jax import lax
from jax.experimental import pallas as pl
from jax.experimental.pallas import tpu as pltpu
from jax.sharding import Mesh
from jax.sharding import PartitionSpec as P


SEQ = ("zl", "y", "x")
SECTION = ("zh", "co")
C = 1536
HALF = C // 2
TAPS = 5
RUN = 1024
EDGE = 12
BLOCK = 96
SHIFTS = (0, 1, -1, 2)
TILES = HALF // 128
GELU = 0.7978845608028654


def up16(rows):
    return -(-rows // 16) * 16


def even_chunk(rows, most):
    total = up16(rows)
    return next(total // n for n in range(1, 99) if total % (16 * n) == 0 and total // n <= most)


def activate(load, par_ref, a_scr, rows, edge, meta_ref):
    def step(i, carry):
        start = pl.multiple_of(i * 16, 16)
        parts = load(start)
        squares = jnp.sum(parts[0] * parts[0] + parts[1] * parts[1], axis=-1, keepdims=True)
        scale = lax.rsqrt(squares * (1.0 / C) + 1e-06)
        for side, part in enumerate(parts):
            value = part * scale * par_ref[0:1, side * HALF : (side + 1) * HALF]
            bent = jnp.tanh(value * (GELU + (GELU * 0.044715) * (value * value)))
            half = 0.5 * value
            value = (half + half * bent).astype(jnp.bfloat16).astype(jnp.float32)
            for t in range(TILES):
                tile = value[:, 128 * t : 128 * t + 128]
                a_scr[side * TILES + t, pl.ds(start + 8, 16)] = tile
        return carry

    lax.fori_loop(0, up16(rows) // 16, step, 0)

    @pl.when(meta_ref[1] == 1)
    def _():
        for t in range(2 * TILES):
            a_scr[t, 8 : 8 + edge] = jnp.zeros((edge, 128), jnp.float32)

    @pl.when(meta_ref[2] == 1)
    def _():
        for t in range(2 * TILES):
            a_scr[t, 8 + rows - edge : 8 + rows] = jnp.zeros((edge, 128), jnp.float32)


def spread(par_ref, a_scr, d_ref, rows):
    chunk = even_chunk(rows, 176)
    for t in range(2 * TILES):
        lanes = slice(128 * t, 128 * t + 128)
        taps = [par_ref[1 + k : 2 + k, lanes] for k in range(TAPS)]

        def step(i, carry):
            start = pl.multiple_of(i * chunk, 16)
            total = taps[0] * a_scr[t, pl.ds(start + 4, chunk)]
            for k in range(1, TAPS):
                total = total + taps[k] * a_scr[t, pl.ds(start + 4 + 2 * k, chunk)]
            d_ref[pl.ds(start, chunk), lanes] = total.astype(jnp.bfloat16)
            return carry

        lax.fori_loop(0, up16(rows) // chunk, step, 0)


def weight_copies(slot, meta_ref, pieces, w_ref, sems):
    copies = []
    for piece in pieces:
        for k in range(4):
            n = len(copies)
            row = pl.multiple_of(meta_ref[3 + n] * BLOCK, 16)
            source = piece.at[k, slot] if len(piece.shape) == 4 else piece.at[k]
            copies.append(
                pltpu.make_async_copy(source, w_ref.at[pl.ds(row, BLOCK)], sems.at[n])
            )
    return copies


def mix_and_pool(d_ref, w_ref, residual, y_scr, out_ref, rows):
    count = (rows - 8) // 2
    total = up16(rows)
    chunk = even_chunk(rows, 272)
    for start in range(0, total, chunk):
        product = jnp.dot(
            d_ref[start : start + chunk], w_ref[...], preferred_element_type=jnp.float32
        )
        mixed = residual(start, chunk) + product
        for n in range(TILES):
            y_scr[n, start : start + chunk] = mixed[:, 128 * n : 128 * n + 128]
    part = next(p for p in (128, 104, 64, 40, 16, 8, 4) if count % p == 0)
    for start in range(0, count, part):
        for n in range(TILES):
            even = y_scr[n, pl.ds(4 + 2 * start, part, stride=2)]
            odd = y_scr[n, pl.ds(5 + 2 * start, part, stride=2)]
            pooled = jnp.maximum(even, odd).astype(jnp.bfloat16)
            out_ref[start : start + part, 128 * n : 128 * n + 128] = pooled


def first_half(rows, meta_ref, hot_ref, stem_ref, par_ref, x_ref, d_ref, x_scr, a_scr):
    chunk = 176
    for start in range(0, up16(rows), chunk):
        for side, target in enumerate((x_ref, x_scr)):
            target[start : start + chunk] = jnp.dot(
                hot_ref[start : start + chunk],
                stem_ref[:, side * HALF : (side + 1) * HALF],
                preferred_element_type=jnp.float32,
            ).astype(jnp.bfloat16)

    def load(start):
        return [ref[pl.ds(start, 16)].astype(jnp.float32) for ref in (x_ref, x_scr)]

    activate(load, par_ref, a_scr, rows, EDGE, meta_ref)
    spread(par_ref, a_scr, d_ref, rows)


def second_half(rows, meta_ref, x_ref, d_ref, *refs):
    *pieces, out_ref, w_ref, y_scr, sems = refs
    copies = weight_copies(0, meta_ref, pieces, w_ref, sems)
    for copy in copies:
        copy.start()
    for copy in copies:
        copy.wait()

    def residual(start, chunk):
        return x_ref[start : start + chunk].astype(jnp.float32)

    mix_and_pool(d_ref, w_ref, residual, y_scr, out_ref, rows)


def swapped_level(rows, edge, meta_ref, own_ref, other_ref, par_ref, *refs):
    *pieces, out_ref, w_ref, a_scr, d_scr, y_scr, sems = refs
    copies = weight_copies(1, meta_ref, pieces, w_ref, sems)
    for copy in copies:
        copy.start()

    def load(start):
        return [ref[pl.ds(start, 16)].astype(jnp.float32) for ref in (own_ref, other_ref)]

    activate(load, par_ref, a_scr, rows, edge, meta_ref)
    spread(par_ref, a_scr, d_scr, rows)
    for copy in copies:
        copy.wait()

    def residual(start, chunk):
        return own_ref[start : start + chunk].astype(jnp.float32)

    mix_and_pool(d_scr, w_ref, residual, y_scr, out_ref, rows)


def paired_level(rows, edge, meta_ref, x_ref, par_ref, w_ref, out_ref, a_scr, d_scr, y_scr):
    own = meta_ref[0]

    def load(start):
        return [x_ref[side, pl.ds(start, 16)].astype(jnp.float32) for side in (own, 1 - own)]

    activate(load, par_ref, a_scr, rows, edge, meta_ref)
    spread(par_ref, a_scr, d_scr, rows)

    def residual(start, chunk):
        return x_ref[own, start : start + chunk].astype(jnp.float32)

    mix_and_pool(d_scr, w_ref, residual, y_scr, out_ref, rows)


def spec(memory_space=pltpu.VMEM):
    return pl.BlockSpec(memory_space=memory_space)


def out_rows(rows, last):
    return (rows - 8) // 2 if last else up16((rows - 8) // 2)


def scratch(rows, names):
    size = up16(rows)
    shapes = {
        "a": pltpu.VMEM((2 * TILES, size + 16, 128), jnp.float32),
        "d": pltpu.VMEM((size, C), jnp.bfloat16),
        "x": pltpu.VMEM((size, HALF), jnp.bfloat16),
        "y": pltpu.VMEM((TILES, size, 128), jnp.float32),
        "s": pltpu.SemaphoreType.DMA((16,)),
    }
    return [shapes[name] for name in names]


def half_rows(size, width=HALF):
    return jax.ShapeDtypeStruct((size, width), jnp.bfloat16)


def run_first_half(rows, meta, hot, stem, par):
    size = up16(rows)
    return pl.pallas_call(
        lambda *refs: first_half(rows, *refs),
        in_specs=[spec(pltpu.SMEM), spec(), spec(), spec()],
        out_specs=[spec(), spec()],
        out_shape=[half_rows(size), half_rows(size, C)],
        scratch_shapes=scratch(rows, "xa"),
        name="stem_and_taps",
    )(meta, hot, stem, par)


def run_second_half(rows, meta, x, d, pieces):
    return pl.pallas_call(
        lambda *refs: second_half(rows, *refs),
        in_specs=[spec(pltpu.SMEM), spec(), spec()] + [spec(pl.ANY)] * len(pieces),
        out_specs=[spec(), spec()],
        out_shape=[half_rows(out_rows(rows, False)), half_rows(C)],
        scratch_shapes=scratch(rows, "ys"),
        name="mix_first",
    )(meta, x, d, *pieces)


def run_swapped_level(rows, edge, meta, own, other, par, pieces):
    return pl.pallas_call(
        lambda *refs: swapped_level(rows, edge, *refs),
        in_specs=[spec(pltpu.SMEM)] + [spec()] * 3 + [spec(pl.ANY)] * len(pieces),
        out_specs=[spec(), spec()],
        out_shape=[half_rows(out_rows(rows, True)), half_rows(C)],
        scratch_shapes=scratch(rows, "adys"),
    )(meta, own, other, par, *pieces)


def run_level(rows, edge, last, meta, x, par, weights):
    return pl.pallas_call(
        lambda *refs: paired_level(rows, edge, *refs),
        in_specs=[spec(pltpu.SMEM)] + [spec()] * 3,
        out_specs=spec(),
        out_shape=half_rows(out_rows(rows, last)),
        scratch_shapes=scratch(rows, "ady"),
    )(meta, x, par, weights)


def ring(size, by):
    return [(i, (i + by) % size) for i in range(size)]


def around_y(array):
    copies = lax.optimization_barrier(jnp.broadcast_to(array[None], (4, *array.shape)))
    return lax.all_to_all(copies, "y", 0, 0, tiled=True)


def own_first(array, co):
    turned = jnp.concatenate([array[..., HALF:], array[..., :HALF]], axis=-1)
    return jnp.where(co == 0, array, turned)


def flat(b, g, role):
    zh, zl, y = 2 * b + g % 2, g // 8, (g // 2) % 4
    return ((zh * 4 + zl) * 4 + y) * 4 + role


def by_role(array):
    pairs = [(r * 4 + zh, zh * 4 + r) for zh in range(4) for r in range(4)]
    return lax.ppermute(array, ("zh", "x"), pairs)


def gathered_bases(bases, sequence):
    mine = lax.dynamic_index_in_dim(bases + 1, sequence, 0, keepdims=False)
    parts = []
    for by in (-1, 0, 1, 2):
        pairs = []
        for zh in range(4):
            for row in range(16):
                place = 4 * row + 2 * (zh % 2) + by
                if 0 <= place < 64:
                    pairs.append((zh * 64 + place, zh * 64 + row * 4))
        parts.append(lax.ppermute(mine, ("zh", "zl", "y", "x"), pairs))
    return parts


def pass_on(array, role):
    rows = array.shape[0]
    axes = ("zh", "zl", "y", "x")
    up = [(flat(b, g, role), flat(b, g + 1, role + 1)) for b in range(2) for g in range(31)]
    down = [(flat(b, g + 1, role), flat(b, g, role + 1)) for b in range(2) for g in range(31)]
    before = lax.ppermute(array[rows - EDGE :], axes, up)
    after = lax.ppermute(array[:EDGE], axes, down)
    own = lax.ppermute(array, "x", [(role, role + 1)])
    blank = jnp.zeros((8, HALF), array.dtype)
    return jnp.concatenate([before, own, after, blank], axis=0)


def relay(bases, stem_weight, gains, depth_taps, point_weight):
    zh, co, zl, y, x = [lax.axis_index(name) for name in ("zh", "co", "zl", "y", "x")]
    margin = stem_weight.shape[0] // 2
    group = (zl * 4 + y) * 2 + zh % 2
    sequence = zh // 2

    rows = RUN + 2 * EDGE
    size = up16(rows)
    ids = gathered_bases(bases, sequence)
    params = jnp.concatenate([gains, depth_taps[0], jnp.zeros((2, C), gains.dtype)], axis=0)
    params = by_role(params)

    held = lax.all_gather(point_weight[0], "zh")
    blocks = held.reshape(4, 24, 2, HALF).transpose(2, 0, 1, 3)
    blocks = jnp.broadcast_to(blocks[:, None], (2, 4, 4, 24, HALF)).reshape(32, 24, HALF)
    blocks = lax.optimization_barrier(blocks)
    blocks = lax.all_to_all(blocks, ("co", "y", "x"), 0, 0, tiled=True)
    near = lax.optimization_barrier(blocks.reshape(2, 4, BLOCK, HALF))
    share = lax.dynamic_index_in_dim(near, y, 1, keepdims=False)
    share0 = lax.ppermute(share[0], ("zh", "zl"), ring(16, 2))
    share1 = lax.ppermute(share[1], ("zh", "zl"), ring(16, -2))
    beside = []
    for slot in range(2):
        sides = [near[slot]]
        for by in (1, -1):
            sides.append(lax.ppermute(near[slot], ("zh", "zl"), ring(16, by)))
        beside.append(sides)
    opposite = around_y(jnp.stack([share0, share1]))
    pieces = [sides + [opposite] for sides in beside]
    params = lax.all_gather(params, "co")
    params = own_first(params, co).astype(jnp.float32)
    four = jnp.arange(4, dtype=jnp.int32)
    z_of = (zl - jnp.array(SHIFTS, jnp.int32)) % 4
    place = (z_of[:, None] * 4 + four[None, :]).reshape(-1)
    flags = jnp.stack([co, (group == 0).astype(jnp.int32), (group == 31).astype(jnp.int32)])
    meta = jnp.concatenate([flags.astype(jnp.int32), (place + 8 * co) % 16])

    ids = jnp.concatenate(ids)[bases.shape[1] - EDGE - margin :][: size + 2 * margin]
    windows = jnp.stack([ids[k : k + size] for k in range(2 * margin + 1)])
    kinds = jnp.arange(1, 5, dtype=jnp.int32)[None, :, None]
    hot = (windows[:, None, :] == kinds).astype(jnp.bfloat16).reshape(-1, size)
    hot = jnp.pad(hot, ((0, 4), (0, 0))).T
    stem = own_first(jnp.pad(stem_weight.reshape(-1, C), ((0, 4), (0, 0))), co)
    level_rows, taps = run_first_half(rows, meta, hot, stem, params[0])
    now, even_weights = run_second_half(rows, meta, level_rows, taps, pieces[0])
    other = lax.ppermute(now, "co", [(0, 1), (1, 0)])
    now, odd_weights = run_swapped_level(
        RUN // 2 + 8, 4, meta, now, other, params[1], pieces[1]
    )
    run = RUN // 4
    for role in range(3):
        now = lax.all_gather(pass_on(now, role), "co")
        now = run_level(run + 2 * EDGE, EDGE, False, meta, now, params[0], even_weights)
        now = lax.all_gather(now, "co")
        now = run_level(run // 2 + 8, 4, True, meta, now, params[1], odd_weights)
        run = run // 4

    blocks = now.reshape(2, 2, 4, HALF // 4).transpose(2, 0, 1, 3)
    blocks = jnp.broadcast_to(
        blocks[None, :, None], (2, 4, 2, 2, 2, HALF // 4)
    ).reshape(32, 2, HALF // 4)
    got = lax.all_to_all(blocks, ("zh", "co", "x"), 0, 0, tiled=True)
    got = got.reshape(2, 2, 2, 4, 2, HALF // 4)[:, :, :, 3]
    got = lax.dynamic_index_in_dim(got, x // 2, 1, keepdims=False)
    return lax.dynamic_index_in_dim(got, zh // 2, 1, keepdims=False)


def solution(mesh):
    finer = Mesh(mesh.devices.reshape(4, 2, 4, 4, 4), SECTION + SEQ)
    in_specs = (
        P(None, SEQ),
        P(),
        P(SECTION, None),
        P(SECTION, None, None),
        P(SECTION, SEQ, None),
    )
    out_specs = P(None, SEQ, SECTION)
    return jax.shard_map(relay, mesh=finer, in_specs=in_specs, out_specs=out_specs, check_vma=False)
```

```python
import jax
import jax.numpy as jnp
from jax import lax
from jax.experimental import pallas as pl
from jax.experimental.pallas import tpu as pltpu
from jax.sharding import Mesh
from jax.sharding import PartitionSpec as P


SEQ = ("zl", "y", "x")
SECTION = ("zh", "co")
C = 1536
HALF = C // 2
TAPS = 5
RUN = 1024
EDGE = 12
BLOCK = 96
SHIFTS = (0, 1, -1, 2)
TILES = HALF // 128
GELU = 0.7978845608028654


def up16(rows):
    return -(-rows // 16) * 16


def even_chunk(rows, most):
    total = up16(rows)
    return next(total // n for n in range(1, 99) if total % (16 * n) == 0 and total // n <= most)


def activate(load, par_ref, a_scr, rows, edge, meta_ref):
    def step(i, carry):
        start = pl.multiple_of(i * 16, 16)
        parts = load(start)
        squares = jnp.sum(parts[0] * parts[0] + parts[1] * parts[1], axis=-1, keepdims=True)
        scale = lax.rsqrt(squares * (1.0 / C) + 1e-06)
        for side, part in enumerate(parts):
            value = part * scale * par_ref[0:1, side * HALF : (side + 1) * HALF]
            bent = jnp.tanh(value * (GELU + (GELU * 0.044715) * (value * value)))
            half = 0.5 * value
            value = (half + half * bent).astype(jnp.bfloat16).astype(jnp.float32)
            for t in range(TILES):
                tile = value[:, 128 * t : 128 * t + 128]
                a_scr[side * TILES + t, pl.ds(start + 8, 16)] = tile
        return carry

    count = up16(rows) // 16
    lax.fori_loop(0, count, step, 0, unroll=3 if count % 3 == 0 else 1)

    @pl.when(meta_ref[1] == 1)
    def _():
        for t in range(2 * TILES):
            a_scr[t, 8 : 8 + edge] = jnp.zeros((edge, 128), jnp.float32)

    @pl.when(meta_ref[2] == 1)
    def _():
        for t in range(2 * TILES):
            a_scr[t, 8 + rows - edge : 8 + rows] = jnp.zeros((edge, 128), jnp.float32)


def spread(par_ref, a_scr, d_ref, rows):
    chunk = even_chunk(rows, 176)
    for t in range(2 * TILES):
        lanes = slice(128 * t, 128 * t + 128)
        taps = [par_ref[1 + k : 2 + k, lanes] for k in range(TAPS)]

        def step(i, carry):
            start = pl.multiple_of(i * chunk, 16)
            total = taps[0] * a_scr[t, pl.ds(start + 4, chunk)]
            for k in range(1, TAPS):
                total = total + taps[k] * a_scr[t, pl.ds(start + 4 + 2 * k, chunk)]
            d_ref[pl.ds(start, chunk), lanes] = total.astype(jnp.bfloat16)
            return carry

        lax.fori_loop(0, up16(rows) // chunk, step, 0)


def weight_copies(slot, meta_ref, pieces, w_ref, sems):
    copies = []
    for piece in pieces:
        for k in range(4):
            n = len(copies)
            row = pl.multiple_of(meta_ref[3 + n] * BLOCK, 16)
            source = piece.at[k, slot] if len(piece.shape) == 4 else piece.at[k]
            copies.append(
                pltpu.make_async_copy(source, w_ref.at[pl.ds(row, BLOCK)], sems.at[n])
            )
    return copies


def mix_and_pool(d_ref, w_ref, residual, y_scr, out_ref, rows):
    count = (rows - 8) // 2
    total = up16(rows)
    chunk = even_chunk(rows, 272)
    for start in range(0, total, chunk):
        product = jnp.dot(
            d_ref[start : start + chunk], w_ref[...], preferred_element_type=jnp.float32
        )
        mixed = residual(start, chunk) + product
        for n in range(TILES):
            y_scr[n, start : start + chunk] = mixed[:, 128 * n : 128 * n + 128]
    part = next(p for p in (128, 104, 64, 40, 16, 8, 4) if count % p == 0)
    for start in range(0, count, part):
        for n in range(TILES):
            even = y_scr[n, pl.ds(4 + 2 * start, part, stride=2)]
            odd = y_scr[n, pl.ds(5 + 2 * start, part, stride=2)]
            pooled = jnp.maximum(even, odd).astype(jnp.bfloat16)
            out_ref[start : start + part, 128 * n : 128 * n + 128] = pooled


def first_half(rows, meta_ref, hot_ref, stem_ref, par_ref, x_ref, d_ref, x_scr, a_scr):
    chunk = 176
    for start in range(0, up16(rows), chunk):
        for side, target in enumerate((x_ref, x_scr)):
            target[start : start + chunk] = jnp.dot(
                hot_ref[start : start + chunk],
                stem_ref[:, side * HALF : (side + 1) * HALF],
                preferred_element_type=jnp.float32,
            ).astype(jnp.bfloat16)

    def load(start):
        return [ref[pl.ds(start, 16)].astype(jnp.float32) for ref in (x_ref, x_scr)]

    activate(load, par_ref, a_scr, rows, EDGE, meta_ref)
    spread(par_ref, a_scr, d_ref, rows)


def second_half(rows, meta_ref, x_ref, d_ref, *refs):
    *pieces, out_ref, w_ref, y_scr, sems = refs
    copies = weight_copies(0, meta_ref, pieces, w_ref, sems)
    for copy in copies:
        copy.start()
    for copy in copies:
        copy.wait()

    def residual(start, chunk):
        return x_ref[start : start + chunk].astype(jnp.float32)

    mix_and_pool(d_ref, w_ref, residual, y_scr, out_ref, rows)


def swapped_level(rows, edge, meta_ref, own_ref, other_ref, par_ref, *refs):
    *pieces, out_ref, w_ref, a_scr, d_scr, y_scr, sems = refs
    copies = weight_copies(1, meta_ref, pieces, w_ref, sems)
    for copy in copies:
        copy.start()

    def load(start):
        return [ref[pl.ds(start, 16)].astype(jnp.float32) for ref in (own_ref, other_ref)]

    activate(load, par_ref, a_scr, rows, edge, meta_ref)
    spread(par_ref, a_scr, d_scr, rows)
    for copy in copies:
        copy.wait()

    def residual(start, chunk):
        return own_ref[start : start + chunk].astype(jnp.float32)

    mix_and_pool(d_scr, w_ref, residual, y_scr, out_ref, rows)


def paired_level(rows, edge, meta_ref, x_ref, par_ref, w_ref, out_ref, a_scr, d_scr, y_scr):
    own = meta_ref[0]

    def load(start):
        return [x_ref[side, pl.ds(start, 16)].astype(jnp.float32) for side in (own, 1 - own)]

    activate(load, par_ref, a_scr, rows, edge, meta_ref)
    spread(par_ref, a_scr, d_scr, rows)

    def residual(start, chunk):
        return x_ref[own, start : start + chunk].astype(jnp.float32)

    mix_and_pool(d_scr, w_ref, residual, y_scr, out_ref, rows)


def spec(memory_space=pltpu.VMEM):
    return pl.BlockSpec(memory_space=memory_space)


def out_rows(rows, last):
    return (rows - 8) // 2 if last else up16((rows - 8) // 2)


def scratch(rows, names):
    size = up16(rows)
    shapes = {
        "a": pltpu.VMEM((2 * TILES, size + 16, 128), jnp.float32),
        "d": pltpu.VMEM((size, C), jnp.bfloat16),
        "x": pltpu.VMEM((size, HALF), jnp.bfloat16),
        "y": pltpu.VMEM((TILES, size, 128), jnp.float32),
        "s": pltpu.SemaphoreType.DMA((16,)),
    }
    return [shapes[name] for name in names]


def half_rows(size, width=HALF):
    return jax.ShapeDtypeStruct((size, width), jnp.bfloat16)


def run_first_half(rows, meta, hot, stem, par):
    size = up16(rows)
    return pl.pallas_call(
        lambda *refs: first_half(rows, *refs),
        in_specs=[spec(pltpu.SMEM), spec(), spec(), spec()],
        out_specs=[spec(), spec()],
        out_shape=[half_rows(size), half_rows(size, C)],
        scratch_shapes=scratch(rows, "xa"),
        name="stem_and_taps",
    )(meta, hot, stem, par)


def run_second_half(rows, meta, x, d, pieces):
    return pl.pallas_call(
        lambda *refs: second_half(rows, *refs),
        in_specs=[spec(pltpu.SMEM), spec(), spec()] + [spec(pl.ANY)] * len(pieces),
        out_specs=[spec(), spec()],
        out_shape=[half_rows(out_rows(rows, False)), half_rows(C)],
        scratch_shapes=scratch(rows, "ys"),
        name="mix_first",
    )(meta, x, d, *pieces)


def run_swapped_level(rows, edge, meta, own, other, par, pieces):
    return pl.pallas_call(
        lambda *refs: swapped_level(rows, edge, *refs),
        in_specs=[spec(pltpu.SMEM)] + [spec()] * 3 + [spec(pl.ANY)] * len(pieces),
        out_specs=[spec(), spec()],
        out_shape=[half_rows(out_rows(rows, True)), half_rows(C)],
        scratch_shapes=scratch(rows, "adys"),
    )(meta, own, other, par, *pieces)


def run_level(rows, edge, last, meta, x, par, weights):
    return pl.pallas_call(
        lambda *refs: paired_level(rows, edge, *refs),
        in_specs=[spec(pltpu.SMEM)] + [spec()] * 3,
        out_specs=spec(),
        out_shape=half_rows(out_rows(rows, last)),
        scratch_shapes=scratch(rows, "ady"),
    )(meta, x, par, weights)


def ring(size, by):
    return [(i, (i + by) % size) for i in range(size)]


def around_y(array):
    copies = lax.optimization_barrier(jnp.broadcast_to(array[None], (4, *array.shape)))
    return lax.all_to_all(copies, "y", 0, 0, tiled=True)


def own_first(array, co):
    turned = jnp.concatenate([array[..., HALF:], array[..., :HALF]], axis=-1)
    return jnp.where(co == 0, array, turned)


def flat(b, g, role):
    zh, zl, y = 2 * b + g % 2, g // 8, (g // 2) % 4
    return ((zh * 4 + zl) * 4 + y) * 4 + role


def gathered_bases(bases, sequence):
    mine = lax.dynamic_index_in_dim(bases + 1, sequence, 0, keepdims=False)
    parts = []
    for by in (-1, 0, 1, 2):
        pairs = []
        for zh in range(4):
            for row in range(16):
                place = 4 * row + 2 * (zh % 2) + by
                if 0 <= place < 64:
                    pairs.append((zh * 64 + place, zh * 64 + row * 4))
        parts.append(lax.ppermute(mine, ("zh", "zl", "y", "x"), pairs))
    return parts


def pass_on(array, role):
    rows = array.shape[0]
    axes = ("zh", "zl", "y", "x")
    up = [(flat(b, g, role), flat(b, g + 1, role + 1)) for b in range(2) for g in range(31)]
    down = [(flat(b, g + 1, role), flat(b, g, role + 1)) for b in range(2) for g in range(31)]
    before = lax.ppermute(array[rows - EDGE :], axes, up)
    after = lax.ppermute(array[:EDGE], axes, down)
    own = lax.ppermute(array, "x", [(role, role + 1)])
    blank = jnp.zeros((8, HALF), array.dtype)
    return jnp.concatenate([before, own, after, blank], axis=0)


def relay(bases, stem_weight, gains, depth_taps, point_weight):
    zh, co, zl, y, x = [lax.axis_index(name) for name in ("zh", "co", "zl", "y", "x")]
    margin = stem_weight.shape[0] // 2
    group = (zl * 4 + y) * 2 + zh % 2
    sequence = zh // 2

    held = [point_weight[0], gains, depth_taps[0], jnp.zeros((2, C), gains.dtype)]
    held = lax.all_gather(jnp.concatenate(held, axis=0), "zh")
    held, bases = lax.optimization_barrier((held, bases))
    ids = gathered_bases(bases, sequence)
    blocks = held[:, :24].reshape(4, 24, 2, HALF).transpose(2, 0, 1, 3)
    blocks = jnp.broadcast_to(blocks[:, None], (2, 4, 4, 24, HALF)).reshape(32, 24, HALF)
    blocks = lax.optimization_barrier(blocks)
    blocks = lax.all_to_all(blocks, ("co", "y", "x"), 0, 0, tiled=True)
    near = lax.optimization_barrier(blocks.reshape(2, 4, BLOCK, HALF))
    share = lax.dynamic_index_in_dim(near, y, 1, keepdims=False)
    share0 = lax.ppermute(share[0], ("zh", "zl"), ring(16, 2))
    share1 = lax.ppermute(share[1], ("zh", "zl"), ring(16, -2))
    beside = []
    for slot in range(2):
        sides = [near[slot]]
        for by in (1, -1):
            sides.append(lax.ppermute(near[slot], ("zh", "zl"), ring(16, by)))
        beside.append(sides)
    opposite = around_y(jnp.stack([share0, share1]))
    pieces = [sides + [opposite] for sides in beside]
    params = lax.dynamic_index_in_dim(held, x, 0, keepdims=False)[24:]
    params = lax.all_gather(params, "co")
    params = own_first(params, co).astype(jnp.float32)
    four = jnp.arange(4, dtype=jnp.int32)
    z_of = (zl - jnp.array(SHIFTS, jnp.int32)) % 4
    place = (z_of[:, None] * 4 + four[None, :]).reshape(-1)
    flags = jnp.stack([co, (group == 0).astype(jnp.int32), (group == 31).astype(jnp.int32)])
    meta = jnp.concatenate([flags.astype(jnp.int32), (place + 8 * co) % 16])

    rows = RUN + 2 * EDGE
    size = up16(rows)
    ids = jnp.concatenate(ids)[bases.shape[1] - EDGE - margin :][: size + 2 * margin]
    windows = jnp.stack([ids[k : k + size] for k in range(2 * margin + 1)])
    kinds = jnp.arange(1, 5, dtype=jnp.int32)[None, :, None]
    hot = (windows[:, None, :] == kinds).astype(jnp.bfloat16).reshape(-1, size)
    hot = jnp.pad(hot, ((0, 4), (0, 0))).T
    stem = own_first(jnp.pad(stem_weight.reshape(-1, C), ((0, 4), (0, 0))), co)
    level_rows, taps = run_first_half(rows, meta, hot, stem, params[0])
    now, even_weights = run_second_half(rows, meta, level_rows, taps, pieces[0])
    other = lax.ppermute(now, "co", [(0, 1), (1, 0)])
    now, odd_weights = run_swapped_level(
        RUN // 2 + 8, 4, meta, now, other, params[1], pieces[1]
    )
    run = RUN // 4
    for role in range(3):
        now = lax.all_gather(pass_on(now, role), "co")
        now = run_level(run + 2 * EDGE, EDGE, False, meta, now, params[0], even_weights)
        now = lax.all_gather(now, "co")
        now = run_level(run // 2 + 8, 4, True, meta, now, params[1], odd_weights)
        run = run // 4

    kept = jnp.zeros((2, HALF), now.dtype)
    for k in range(2):
        for p in range(2):
            pairs = [
                (((2 * b + h) * 2 + c) * 4 + 3, ((2 * c + k) * 2 + b) * 4 + 2 * h + p)
                for b in range(2)
                for h in range(2)
                for c in range(2)
            ]
            kept = kept + lax.ppermute(now[2 * p : 2 * p + 2], ("zh", "co", "x"), pairs)
    kept = lax.all_gather(kept, "co").reshape(2, 2, 4, HALF // 4)
    return lax.dynamic_index_in_dim(kept, (zh % 2) * 2 + co, 2, keepdims=False)


def solution(mesh):
    finer = Mesh(mesh.devices.reshape(4, 2, 4, 4, 4), SECTION + SEQ)
    in_specs = (
        P(None, SEQ),
        P(),
        P(SECTION, None),
        P(SECTION, None, None),
        P(SECTION, SEQ, None),
    )
    out_specs = P(None, SEQ, SECTION)
    return jax.shard_map(relay, mesh=finer, in_specs=in_specs, out_specs=out_specs, check_vma=False)
```

```python
import jax
import jax.numpy as jnp
from jax import lax
from jax.experimental import pallas as pl
from jax.experimental.pallas import tpu as pltpu
from jax.sharding import Mesh
from jax.sharding import PartitionSpec as P


SEQ = ("zl", "y", "x")
SECTION = ("zh", "co")
C = 1536
HALF = C // 2
TAPS = 5
RUN = 1024
EDGE = 12
BLOCK = 96
SHIFTS = (0, 1, -1, 2)
TILES = HALF // 128
GELU = 0.7978845608028654
GRANT = pltpu.CompilerParams(vmem_limit_bytes=24 << 20)


def up16(rows):
    return -(-rows // 16) * 16


def even_chunk(rows, most):
    total = up16(rows)
    return next(total // n for n in range(1, 99) if total % (16 * n) == 0 and total // n <= most)


def activate(load, par_ref, a_scr, rows, edge, meta_ref):
    def step(i, carry):
        start = pl.multiple_of(i * 16, 16)
        parts = load(start)
        squares = jnp.sum(parts[0] * parts[0] + parts[1] * parts[1], axis=-1, keepdims=True)
        scale = lax.rsqrt(squares * (1.0 / C) + 1e-06)
        for side, part in enumerate(parts):
            value = part * scale * par_ref[0:1, side * HALF : (side + 1) * HALF]
            bent = jnp.tanh(value * (GELU + (GELU * 0.044715) * (value * value)))
            half = 0.5 * value
            value = (half + half * bent).astype(jnp.bfloat16).astype(jnp.float32)
            for t in range(TILES):
                tile = value[:, 128 * t : 128 * t + 128]
                a_scr[side * TILES + t, pl.ds(start + 8, 16)] = tile
        return carry

    count = up16(rows) // 16
    lax.fori_loop(0, count, step, 0, unroll=next(n for n in (11, 9, 6, 3, 1) if count % n == 0))

    @pl.when(meta_ref[1] == 1)
    def _():
        for t in range(2 * TILES):
            a_scr[t, 8 : 8 + edge] = jnp.zeros((edge, 128), jnp.float32)

    @pl.when(meta_ref[2] == 1)
    def _():
        for t in range(2 * TILES):
            a_scr[t, 8 + rows - edge : 8 + rows] = jnp.zeros((edge, 128), jnp.float32)


def spread(par_ref, a_scr, d_ref, rows):
    chunk = even_chunk(rows, 176)
    for t in range(2 * TILES):
        lanes = slice(128 * t, 128 * t + 128)
        taps = [par_ref[1 + k : 2 + k, lanes] for k in range(TAPS)]

        def step(i, carry):
            start = pl.multiple_of(i * chunk, 16)
            total = taps[0] * a_scr[t, pl.ds(start + 4, chunk)]
            for k in range(1, TAPS):
                total = total + taps[k] * a_scr[t, pl.ds(start + 4 + 2 * k, chunk)]
            d_ref[pl.ds(start, chunk), lanes] = total.astype(jnp.bfloat16)
            return carry

        lax.fori_loop(0, up16(rows) // chunk, step, 0)


def weight_copies(slot, meta_ref, pieces, w_ref, sems):
    copies = []
    for piece in pieces:
        for k in range(4):
            n = len(copies)
            row = pl.multiple_of(meta_ref[3 + n] * BLOCK, 16)
            source = piece.at[k, slot] if len(piece.shape) == 4 else piece.at[k]
            copies.append(
                pltpu.make_async_copy(source, w_ref.at[pl.ds(row, BLOCK)], sems.at[n])
            )
    return copies


def mix_and_pool(d_ref, w_ref, residual, y_scr, out_ref, rows):
    count = (rows - 8) // 2
    total = up16(rows)
    chunk = even_chunk(rows, 272)
    for start in range(0, total, chunk):
        product = jnp.dot(
            d_ref[start : start + chunk], w_ref[...], preferred_element_type=jnp.float32
        )
        mixed = residual(start, chunk) + product
        for n in range(TILES):
            y_scr[n, start : start + chunk] = mixed[:, 128 * n : 128 * n + 128]
    part = next(p for p in (128, 104, 64, 40, 16, 8, 4) if count % p == 0)
    for start in range(0, count, part):
        for n in range(TILES):
            even = y_scr[n, pl.ds(4 + 2 * start, part, stride=2)]
            odd = y_scr[n, pl.ds(5 + 2 * start, part, stride=2)]
            pooled = jnp.maximum(even, odd).astype(jnp.bfloat16)
            out_ref[start : start + part, 128 * n : 128 * n + 128] = pooled


def first_half(rows, meta_ref, hot_ref, stem_ref, par_ref, x_ref, d_ref, x_scr, a_scr):
    chunk = 176
    for start in range(0, up16(rows), chunk):
        for side, target in enumerate((x_ref, x_scr)):
            target[start : start + chunk] = jnp.dot(
                hot_ref[start : start + chunk],
                stem_ref[:, side * HALF : (side + 1) * HALF],
                preferred_element_type=jnp.float32,
            ).astype(jnp.bfloat16)

    def load(start):
        return [ref[pl.ds(start, 16)].astype(jnp.float32) for ref in (x_ref, x_scr)]

    activate(load, par_ref, a_scr, rows, EDGE, meta_ref)
    spread(par_ref, a_scr, d_ref, rows)


def second_half(rows, meta_ref, x_ref, d_ref, *refs):
    *pieces, out_ref, w_ref, y_scr, sems = refs
    copies = weight_copies(0, meta_ref, pieces, w_ref, sems)
    for copy in copies:
        copy.start()
    for copy in copies:
        copy.wait()

    def residual(start, chunk):
        return x_ref[start : start + chunk].astype(jnp.float32)

    mix_and_pool(d_ref, w_ref, residual, y_scr, out_ref, rows)


def swapped_level(rows, edge, meta_ref, own_ref, other_ref, par_ref, *refs):
    *pieces, out_ref, w_ref, a_scr, d_scr, y_scr, sems = refs
    copies = weight_copies(1, meta_ref, pieces, w_ref, sems)
    for copy in copies:
        copy.start()

    def load(start):
        return [ref[pl.ds(start, 16)].astype(jnp.float32) for ref in (own_ref, other_ref)]

    activate(load, par_ref, a_scr, rows, edge, meta_ref)
    spread(par_ref, a_scr, d_scr, rows)
    for copy in copies:
        copy.wait()

    def residual(start, chunk):
        return own_ref[start : start + chunk].astype(jnp.float32)

    mix_and_pool(d_scr, w_ref, residual, y_scr, out_ref, rows)


def paired_level(rows, edge, meta_ref, x_ref, par_ref, w_ref, out_ref, a_scr, d_scr, y_scr):
    own = meta_ref[0]

    def load(start):
        return [x_ref[side, pl.ds(start, 16)].astype(jnp.float32) for side in (own, 1 - own)]

    activate(load, par_ref, a_scr, rows, edge, meta_ref)
    spread(par_ref, a_scr, d_scr, rows)

    def residual(start, chunk):
        return x_ref[own, start : start + chunk].astype(jnp.float32)

    mix_and_pool(d_scr, w_ref, residual, y_scr, out_ref, rows)


def spec(memory_space=pltpu.VMEM):
    return pl.BlockSpec(memory_space=memory_space)


def out_rows(rows, last):
    return (rows - 8) // 2 if last else up16((rows - 8) // 2)


def scratch(rows, names):
    size = up16(rows)
    shapes = {
        "a": pltpu.VMEM((2 * TILES, size + 16, 128), jnp.float32),
        "d": pltpu.VMEM((size, C), jnp.bfloat16),
        "x": pltpu.VMEM((size, HALF), jnp.bfloat16),
        "y": pltpu.VMEM((TILES, size, 128), jnp.float32),
        "s": pltpu.SemaphoreType.DMA((16,)),
    }
    return [shapes[name] for name in names]


def half_rows(size, width=HALF):
    return jax.ShapeDtypeStruct((size, width), jnp.bfloat16)


def run_first_half(rows, meta, hot, stem, par):
    size = up16(rows)
    return pl.pallas_call(
        lambda *refs: first_half(rows, *refs),
        in_specs=[spec(pltpu.SMEM), spec(), spec(), spec()],
        out_specs=[spec(), spec()],
        out_shape=[half_rows(size), half_rows(size, C)],
        scratch_shapes=scratch(rows, "xa"),
        name="stem_and_taps",
    )(meta, hot, stem, par)


def run_second_half(rows, meta, x, d, pieces):
    return pl.pallas_call(
        lambda *refs: second_half(rows, *refs),
        in_specs=[spec(pltpu.SMEM), spec(), spec()] + [spec(pl.ANY)] * len(pieces),
        out_specs=[spec(), spec()],
        out_shape=[half_rows(out_rows(rows, False)), half_rows(C)],
        scratch_shapes=scratch(rows, "ys"),
        compiler_params=GRANT,
        name="mix_first",
    )(meta, x, d, *pieces)


def run_swapped_level(rows, edge, meta, own, other, par, pieces):
    return pl.pallas_call(
        lambda *refs: swapped_level(rows, edge, *refs),
        in_specs=[spec(pltpu.SMEM)] + [spec()] * 3 + [spec(pl.ANY)] * len(pieces),
        out_specs=[spec(), spec()],
        out_shape=[half_rows(out_rows(rows, True)), half_rows(C)],
        scratch_shapes=scratch(rows, "adys"),
        compiler_params=GRANT,
    )(meta, own, other, par, *pieces)


def run_level(rows, edge, last, meta, x, par, weights):
    return pl.pallas_call(
        lambda *refs: paired_level(rows, edge, *refs),
        in_specs=[spec(pltpu.SMEM)] + [spec()] * 3,
        out_specs=spec(),
        out_shape=half_rows(out_rows(rows, last)),
        scratch_shapes=scratch(rows, "ady"),
        compiler_params=GRANT,
    )(meta, x, par, weights)


def ring(size, by):
    return [(i, (i + by) % size) for i in range(size)]


def around_y(array):
    copies = lax.optimization_barrier(jnp.broadcast_to(array[None], (4, *array.shape)))
    return lax.all_to_all(copies, "y", 0, 0, tiled=True)


def own_first(array, co):
    turned = jnp.concatenate([array[..., HALF:], array[..., :HALF]], axis=-1)
    return jnp.where(co == 0, array, turned)


def flat(b, g, role):
    zh, zl, y = 2 * b + g % 2, g // 8, (g // 2) % 4
    return ((zh * 4 + zl) * 4 + y) * 4 + role


def gathered_bases(bases, sequence):
    mine = lax.dynamic_index_in_dim(bases + 1, sequence, 0, keepdims=False)
    parts = []
    for by in (-1, 0, 1, 2):
        pairs = []
        for zh in range(4):
            for row in range(16):
                place = 4 * row + 2 * (zh % 2) + by
                if 0 <= place < 64:
                    pairs.append((zh * 64 + place, zh * 64 + row * 4))
        parts.append(lax.ppermute(mine, ("zh", "zl", "y", "x"), pairs))
    return parts


def pass_on(array, role):
    rows = array.shape[0]
    axes = ("zh", "zl", "y", "x")
    up = [(flat(b, g, role), flat(b, g + 1, role + 1)) for b in range(2) for g in range(31)]
    down = [(flat(b, g + 1, role), flat(b, g, role + 1)) for b in range(2) for g in range(31)]
    before = lax.ppermute(array[rows - EDGE :], axes, up)
    after = lax.ppermute(array[:EDGE], axes, down)
    own = lax.ppermute(array, "x", [(role, role + 1)])
    blank = jnp.zeros((8, HALF), array.dtype)
    return jnp.concatenate([before, own, after, blank], axis=0)


def relay(bases, stem_weight, gains, depth_taps, point_weight):
    zh, co, zl, y, x = [lax.axis_index(name) for name in ("zh", "co", "zl", "y", "x")]
    margin = stem_weight.shape[0] // 2
    group = (zl * 4 + y) * 2 + zh % 2
    sequence = zh // 2

    held = [point_weight[0], gains, depth_taps[0], jnp.zeros((2, C), gains.dtype)]
    held = lax.all_gather(jnp.concatenate(held, axis=0), "zh")
    held, bases = lax.optimization_barrier((held, bases))
    ids = gathered_bases(bases, sequence)
    blocks = held[:, :24].reshape(4, 24, 2, HALF).transpose(2, 0, 1, 3)
    blocks = jnp.broadcast_to(blocks[:, None], (2, 4, 4, 24, HALF)).reshape(32, 24, HALF)
    blocks = lax.optimization_barrier(blocks)
    blocks = lax.all_to_all(blocks, ("co", "y", "x"), 0, 0, tiled=True)
    near = lax.optimization_barrier(blocks.reshape(2, 4, BLOCK, HALF))
    share = lax.dynamic_index_in_dim(near, y, 1, keepdims=False)
    share0 = lax.ppermute(share[0], ("zh", "zl"), ring(16, 2))
    share1 = lax.ppermute(share[1], ("zh", "zl"), ring(16, -2))
    beside = []
    for slot in range(2):
        sides = [near[slot]]
        for by in (1, -1):
            sides.append(lax.ppermute(near[slot], ("zh", "zl"), ring(16, by)))
        beside.append(sides)
    opposite = around_y(jnp.stack([share0, share1]))
    pieces = [sides + [opposite] for sides in beside]
    params = lax.dynamic_index_in_dim(held, x, 0, keepdims=False)[24:]
    params = lax.all_gather(params, "co")
    params = own_first(params, co).astype(jnp.float32)
    four = jnp.arange(4, dtype=jnp.int32)
    z_of = (zl - jnp.array(SHIFTS, jnp.int32)) % 4
    place = (z_of[:, None] * 4 + four[None, :]).reshape(-1)
    flags = jnp.stack([co, (group == 0).astype(jnp.int32), (group == 31).astype(jnp.int32)])
    meta = jnp.concatenate([flags.astype(jnp.int32), (place + 8 * co) % 16])

    rows = RUN + 2 * EDGE
    size = up16(rows)
    ids = jnp.concatenate(ids)[bases.shape[1] - EDGE - margin :][: size + 2 * margin]
    windows = jnp.stack([ids[k : k + size] for k in range(2 * margin + 1)])
    kinds = jnp.arange(1, 5, dtype=jnp.int32)[None, :, None]
    hot = (windows[:, None, :] == kinds).astype(jnp.bfloat16).reshape(-1, size)
    hot = jnp.pad(hot, ((0, 4), (0, 0))).T
    stem = own_first(jnp.pad(stem_weight.reshape(-1, C), ((0, 4), (0, 0))), co)
    level_rows, taps = run_first_half(rows, meta, hot, stem, params[0])
    now, even_weights = run_second_half(rows, meta, level_rows, taps, pieces[0])
    other = lax.ppermute(now, "co", [(0, 1), (1, 0)])
    now, odd_weights = run_swapped_level(
        RUN // 2 + 8, 4, meta, now, other, params[1], pieces[1]
    )
    run = RUN // 4
    for role in range(3):
        now = lax.all_gather(pass_on(now, role), "co")
        now = run_level(run + 2 * EDGE, EDGE, False, meta, now, params[0], even_weights)
        now = lax.all_gather(now, "co")
        now = run_level(run // 2 + 8, 4, True, meta, now, params[1], odd_weights)
        run = run // 4

    kept = jnp.zeros((2, HALF), now.dtype)
    for k in range(2):
        for p in range(2):
            pairs = [
                (((2 * b + h) * 2 + c) * 4 + 3, ((2 * c + k) * 2 + b) * 4 + 2 * h + p)
                for b in range(2)
                for h in range(2)
                for c in range(2)
            ]
            kept = kept + lax.ppermute(now[2 * p : 2 * p + 2], ("zh", "co", "x"), pairs)
    kept = lax.all_gather(kept, "co").reshape(2, 2, 4, HALF // 4)
    return lax.dynamic_index_in_dim(kept, (zh % 2) * 2 + co, 2, keepdims=False)


def solution(mesh):
    finer = Mesh(mesh.devices.reshape(4, 2, 4, 4, 4), SECTION + SEQ)
    in_specs = (
        P(None, SEQ),
        P(),
        P(SECTION, None),
        P(SECTION, None, None),
        P(SECTION, SEQ, None),
    )
    out_specs = P(None, SEQ, SECTION)
    return jax.shard_map(relay, mesh=finer, in_specs=in_specs, out_specs=out_specs, check_vma=False)
```

```python
import jax
import jax.numpy as jnp
from jax import lax
from jax.experimental import pallas as pl
from jax.experimental.pallas import tpu as pltpu
from jax.sharding import Mesh
from jax.sharding import PartitionSpec as P


SEQ = ("zl", "y", "x")
SECTION = ("zh", "co")
C = 1536
HALF = C // 2
TAPS = 5
RUN = 1024
EDGE = 12
BLOCK = 96
SHIFTS = (0, 1, -1, 2)
TILES = HALF // 128
GELU = 0.7978845608028654
GRANT = pltpu.CompilerParams(vmem_limit_bytes=24 << 20)


def up16(rows):
    return -(-rows // 16) * 16


def even_chunk(rows, most):
    total = up16(rows)
    return next(total // n for n in range(1, 99) if total % (16 * n) == 0 and total // n <= most)


def activate(load, par_ref, a_scr, rows, edge, meta_ref):
    def step(i, carry):
        start = pl.multiple_of(i * 16, 16)
        parts = load(start)
        squares = jnp.sum(parts[0] * parts[0] + parts[1] * parts[1], axis=-1, keepdims=True)
        scale = lax.rsqrt(squares * (1.0 / C) + 1e-06)
        for side, part in enumerate(parts):
            value = part * scale * par_ref[0:1, side * HALF : (side + 1) * HALF]
            bent = jnp.tanh(value * (GELU + (GELU * 0.044715) * (value * value)))
            half = 0.5 * value
            value = (half + half * bent).astype(jnp.bfloat16).astype(jnp.float32)
            for t in range(TILES):
                tile = value[:, 128 * t : 128 * t + 128]
                a_scr[side * TILES + t, pl.ds(start + 8, 16)] = tile
        return carry

    count = up16(rows) // 16
    lax.fori_loop(0, count, step, 0, unroll=next(n for n in (11, 9, 6, 3, 1) if count % n == 0))

    @pl.when(meta_ref[1] == 1)
    def _():
        for t in range(2 * TILES):
            a_scr[t, 8 : 8 + edge] = jnp.zeros((edge, 128), jnp.float32)

    @pl.when(meta_ref[2] == 1)
    def _():
        for t in range(2 * TILES):
            a_scr[t, 8 + rows - edge : 8 + rows] = jnp.zeros((edge, 128), jnp.float32)


def spread(par_ref, a_scr, d_ref, rows):
    chunk = even_chunk(rows, 176)
    for t in range(2 * TILES):
        lanes = slice(128 * t, 128 * t + 128)
        taps = [par_ref[1 + k : 2 + k, lanes] for k in range(TAPS)]

        def step(i, carry):
            start = pl.multiple_of(i * chunk, 16)
            total = taps[0] * a_scr[t, pl.ds(start + 4, chunk)]
            for k in range(1, TAPS):
                total = total + taps[k] * a_scr[t, pl.ds(start + 4 + 2 * k, chunk)]
            d_ref[pl.ds(start, chunk), lanes] = total.astype(jnp.bfloat16)
            return carry

        lax.fori_loop(0, up16(rows) // chunk, step, 0)


def weight_copies(slot, meta_ref, pieces, w_ref, sems):
    copies = []
    for piece in pieces:
        for k in range(4):
            n = len(copies)
            row = pl.multiple_of(meta_ref[3 + n] * BLOCK, 16)
            source = piece.at[k, slot] if len(piece.shape) == 4 else piece.at[k]
            copies.append(
                pltpu.make_async_copy(source, w_ref.at[pl.ds(row, BLOCK)], sems.at[n])
            )
    return copies


def mix_and_pool(d_ref, w_ref, residual, y_scr, out_ref, rows):
    count = (rows - 8) // 2
    total = up16(rows)
    chunk = even_chunk(rows, 272)
    for start in range(0, total, chunk):
        product = jnp.dot(
            d_ref[start : start + chunk], w_ref[...], preferred_element_type=jnp.float32
        )
        mixed = residual(start, chunk) + product
        for n in range(TILES):
            y_scr[n, start : start + chunk] = mixed[:, 128 * n : 128 * n + 128]
    part = next(p for p in (128, 104, 64, 40, 16, 8, 4) if count % p == 0)
    for start in range(0, count, part):
        for n in range(TILES):
            even = y_scr[n, pl.ds(4 + 2 * start, part, stride=2)]
            odd = y_scr[n, pl.ds(5 + 2 * start, part, stride=2)]
            pooled = jnp.maximum(even, odd).astype(jnp.bfloat16)
            out_ref[start : start + part, 128 * n : 128 * n + 128] = pooled


def first_half(rows, meta_ref, hot_ref, stem_ref, par_ref, x_ref, d_ref, x_scr, a_scr):
    chunk = 176
    for start in range(0, up16(rows), chunk):
        for side, target in enumerate((x_ref, x_scr)):
            target[start : start + chunk] = jnp.dot(
                hot_ref[start : start + chunk],
                stem_ref[:, side * HALF : (side + 1) * HALF],
                preferred_element_type=jnp.float32,
            ).astype(jnp.bfloat16)

    def load(start):
        return [ref[pl.ds(start, 16)].astype(jnp.float32) for ref in (x_ref, x_scr)]

    activate(load, par_ref, a_scr, rows, EDGE, meta_ref)
    spread(par_ref, a_scr, d_ref, rows)


def second_half(rows, meta_ref, x_hbm, d_hbm, *refs):
    *pieces, out_ref, w_ref, x_scr, d_scr, y_scr, sems, row_sems = refs
    copies = weight_copies(0, meta_ref, pieces, w_ref, sems)
    copies.append(pltpu.make_async_copy(d_hbm, d_scr, row_sems.at[0]))
    copies.append(pltpu.make_async_copy(x_hbm, x_scr, row_sems.at[1]))
    for copy in copies:
        copy.start()
    for copy in copies:
        copy.wait()

    def residual(start, chunk):
        return x_scr[start : start + chunk].astype(jnp.float32)

    mix_and_pool(d_scr, w_ref, residual, y_scr, out_ref, rows)


def assemble(slot, meta_ref, *refs):
    *pieces, w_ref, sems = refs
    copies = weight_copies(slot, meta_ref, pieces, w_ref, sems)
    for copy in copies:
        copy.start()
    for copy in copies:
        copy.wait()


def swapped_level(
    rows, edge, meta_ref, own_ref, other_ref, par_ref, w_ref, out_ref, a_scr, d_scr, y_scr
):
    def load(start):
        return [ref[pl.ds(start, 16)].astype(jnp.float32) for ref in (own_ref, other_ref)]

    activate(load, par_ref, a_scr, rows, edge, meta_ref)
    spread(par_ref, a_scr, d_scr, rows)

    def residual(start, chunk):
        return own_ref[start : start + chunk].astype(jnp.float32)

    mix_and_pool(d_scr, w_ref, residual, y_scr, out_ref, rows)


def paired_level(rows, edge, meta_ref, x_ref, par_ref, w_ref, out_ref, a_scr, d_scr, y_scr):
    own = meta_ref[0]

    def load(start):
        return [x_ref[side, pl.ds(start, 16)].astype(jnp.float32) for side in (own, 1 - own)]

    activate(load, par_ref, a_scr, rows, edge, meta_ref)
    spread(par_ref, a_scr, d_scr, rows)

    def residual(start, chunk):
        return x_ref[own, start : start + chunk].astype(jnp.float32)

    mix_and_pool(d_scr, w_ref, residual, y_scr, out_ref, rows)


def spec(memory_space=pltpu.VMEM):
    return pl.BlockSpec(memory_space=memory_space)


def out_rows(rows, last):
    return (rows - 8) // 2 if last else up16((rows - 8) // 2)


def scratch(rows, names):
    size = up16(rows)
    shapes = {
        "a": pltpu.VMEM((2 * TILES, size + 16, 128), jnp.float32),
        "d": pltpu.VMEM((size, C), jnp.bfloat16),
        "x": pltpu.VMEM((size, HALF), jnp.bfloat16),
        "y": pltpu.VMEM((TILES, size, 128), jnp.float32),
        "s": pltpu.SemaphoreType.DMA((16,)),
        "r": pltpu.SemaphoreType.DMA((2,)),
    }
    return [shapes[name] for name in names]


def half_rows(size, width=HALF):
    return jax.ShapeDtypeStruct((size, width), jnp.bfloat16)


def run_first_half(rows, meta, hot, stem, par):
    size = up16(rows)
    return pl.pallas_call(
        lambda *refs: first_half(rows, *refs),
        in_specs=[spec(pltpu.SMEM), spec(), spec(), spec()],
        out_specs=[spec(), spec()],
        out_shape=[half_rows(size), half_rows(size, C)],
        scratch_shapes=scratch(rows, "xa"),
        name="stem_and_taps",
    )(meta, hot, stem, par)


def run_second_half(rows, meta, x, d, pieces):
    return pl.pallas_call(
        lambda *refs: second_half(rows, *refs),
        in_specs=[spec(pltpu.SMEM), spec(pltpu.HBM), spec(pltpu.HBM)] + [spec(pl.ANY)] * len(pieces),
        out_specs=[spec(), spec()],
        out_shape=[half_rows(out_rows(rows, False)), half_rows(C)],
        scratch_shapes=scratch(rows, "xdysr"),
        compiler_params=GRANT,
        name="mix_first",
    )(meta, *(pltpu.with_memory_space_constraint(part, pltpu.HBM) for part in (x, d)), *pieces)


def run_assemble(slot, meta, pieces):
    return pl.pallas_call(
        lambda *refs: assemble(slot, *refs),
        in_specs=[spec(pltpu.SMEM)] + [spec(pl.ANY)] * len(pieces),
        out_specs=spec(),
        out_shape=half_rows(C),
        scratch_shapes=scratch(16, "s"),
        compiler_params=GRANT,
        name="assemble",
    )(meta, *pieces)


def run_swapped_level(rows, edge, meta, own, other, par, weights):
    return pl.pallas_call(
        lambda *refs: swapped_level(rows, edge, *refs),
        in_specs=[spec(pltpu.SMEM)] + [spec()] * 4,
        out_specs=spec(),
        out_shape=half_rows(out_rows(rows, True)),
        scratch_shapes=scratch(rows, "ady"),
        compiler_params=GRANT,
    )(meta, own, other, par, weights)


def run_level(rows, edge, last, meta, x, par, weights):
    return pl.pallas_call(
        lambda *refs: paired_level(rows, edge, *refs),
        in_specs=[spec(pltpu.SMEM)] + [spec()] * 3,
        out_specs=spec(),
        out_shape=half_rows(out_rows(rows, last)),
        scratch_shapes=scratch(rows, "ady"),
        compiler_params=GRANT,
    )(meta, x, par, weights)


def ring(size, by):
    return [(i, (i + by) % size) for i in range(size)]


def around_y(array):
    copies = lax.optimization_barrier(jnp.broadcast_to(array[None], (4, *array.shape)))
    return lax.all_to_all(copies, "y", 0, 0, tiled=True)


def own_first(array, co):
    turned = jnp.concatenate([array[..., HALF:], array[..., :HALF]], axis=-1)
    return jnp.where(co == 0, array, turned)


def flat(b, g, role):
    zh, zl, y = 2 * b + g % 2, g // 8, (g // 2) % 4
    return ((zh * 4 + zl) * 4 + y) * 4 + role


def gathered_bases(bases, sequence):
    mine = lax.dynamic_index_in_dim(bases + 1, sequence, 0, keepdims=False)
    parts = []
    for by in (-1, 0, 1, 2):
        pairs = []
        for zh in range(4):
            for row in range(16):
                place = 4 * row + 2 * (zh % 2) + by
                if 0 <= place < 64:
                    pairs.append((zh * 64 + place, zh * 64 + row * 4))
        parts.append(lax.ppermute(mine, ("zh", "zl", "y", "x"), pairs))
    return parts


def pass_on(array, role):
    rows = array.shape[0]
    axes = ("zh", "zl", "y", "x")
    up = [(flat(b, g, role), flat(b, g + 1, role + 1)) for b in range(2) for g in range(31)]
    down = [(flat(b, g + 1, role), flat(b, g, role + 1)) for b in range(2) for g in range(31)]
    before = lax.ppermute(array[rows - EDGE :], axes, up)
    after = lax.ppermute(array[:EDGE], axes, down)
    own = lax.ppermute(array, "x", [(role, role + 1)])
    blank = jnp.zeros((8, HALF), array.dtype)
    return jnp.concatenate([before, own, after, blank], axis=0)


def relay(bases, stem_weight, gains, depth_taps, point_weight):
    zh, co, zl, y, x = [lax.axis_index(name) for name in ("zh", "co", "zl", "y", "x")]
    margin = stem_weight.shape[0] // 2
    group = (zl * 4 + y) * 2 + zh % 2
    sequence = zh // 2

    held = [point_weight[0], gains, depth_taps[0], jnp.zeros((2, C), gains.dtype)]
    held = lax.all_gather(jnp.concatenate(held, axis=0), "zh")
    held, bases = lax.optimization_barrier((held, bases))
    ids = gathered_bases(bases, sequence)
    blocks = held[:, :24].reshape(4, 24, 2, HALF).transpose(2, 0, 1, 3)
    blocks = jnp.broadcast_to(blocks[:, None], (2, 4, 4, 24, HALF)).reshape(32, 24, HALF)
    blocks = lax.optimization_barrier(blocks)
    blocks = lax.all_to_all(blocks, ("co", "y", "x"), 0, 0, tiled=True)
    near = lax.optimization_barrier(blocks.reshape(2, 4, BLOCK, HALF))
    share = lax.dynamic_index_in_dim(near, y, 1, keepdims=False)
    share0 = lax.ppermute(share[0], ("zh", "zl"), ring(16, 2))
    share1 = lax.ppermute(share[1], ("zh", "zl"), ring(16, -2))
    beside = []
    for slot in range(2):
        sides = [near[slot]]
        for by in (1, -1):
            sides.append(lax.ppermute(near[slot], ("zh", "zl"), ring(16, by)))
        beside.append(sides)
    opposite = around_y(jnp.stack([share0, share1]))
    pieces = [sides + [opposite] for sides in beside]
    params = lax.dynamic_index_in_dim(held, x, 0, keepdims=False)[24:]
    params = lax.all_gather(params, "co")
    params = own_first(params, co).astype(jnp.float32)
    four = jnp.arange(4, dtype=jnp.int32)
    z_of = (zl - jnp.array(SHIFTS, jnp.int32)) % 4
    place = (z_of[:, None] * 4 + four[None, :]).reshape(-1)
    flags = jnp.stack([co, (group == 0).astype(jnp.int32), (group == 31).astype(jnp.int32)])
    meta = jnp.concatenate([flags.astype(jnp.int32), (place + 8 * co) % 16])

    rows = RUN + 2 * EDGE
    size = up16(rows)
    ids = jnp.concatenate(ids)[bases.shape[1] - EDGE - margin :][: size + 2 * margin]
    windows = jnp.stack([ids[k : k + size] for k in range(2 * margin + 1)])
    kinds = jnp.arange(1, 5, dtype=jnp.int32)[None, :, None]
    hot = (windows[:, None, :] == kinds).astype(jnp.bfloat16).reshape(-1, size)
    hot = jnp.pad(hot, ((0, 4), (0, 0))).T
    stem = own_first(jnp.pad(stem_weight.reshape(-1, C), ((0, 4), (0, 0))), co)
    level_rows, taps = run_first_half(rows, meta, hot, stem, params[0])
    now, even_weights = run_second_half(rows, meta, level_rows, taps, pieces[0])
    other = lax.ppermute(now, "co", [(0, 1), (1, 0)])
    odd_weights = run_assemble(1, meta, pieces[1])
    now = run_swapped_level(RUN // 2 + 8, 4, meta, now, other, params[1], odd_weights)
    run = RUN // 4
    for role in range(3):
        now = lax.all_gather(pass_on(now, role), "co")
        now = run_level(run + 2 * EDGE, EDGE, False, meta, now, params[0], even_weights)
        now = lax.all_gather(now, "co")
        now = run_level(run // 2 + 8, 4, True, meta, now, params[1], odd_weights)
        run = run // 4

    kept = jnp.zeros((2, HALF), now.dtype)
    for k in range(2):
        for p in range(2):
            pairs = [
                (((2 * b + h) * 2 + c) * 4 + 3, ((2 * c + k) * 2 + b) * 4 + 2 * h + p)
                for b in range(2)
                for h in range(2)
                for c in range(2)
            ]
            kept = kept + lax.ppermute(now[2 * p : 2 * p + 2], ("zh", "co", "x"), pairs)
    kept = lax.all_gather(kept, "co").reshape(2, 2, 4, HALF // 4)
    return lax.dynamic_index_in_dim(kept, (zh % 2) * 2 + co, 2, keepdims=False)


def solution(mesh):
    finer = Mesh(mesh.devices.reshape(4, 2, 4, 4, 4), SECTION + SEQ)
    in_specs = (
        P(None, SEQ),
        P(),
        P(SECTION, None),
        P(SECTION, None, None),
        P(SECTION, SEQ, None),
    )
    out_specs = P(None, SEQ, SECTION)
    return jax.shard_map(relay, mesh=finer, in_specs=in_specs, out_specs=out_specs, check_vma=False)
```

```python
import jax
import jax.numpy as jnp
from jax import lax
from jax.experimental import pallas as pl
from jax.experimental.pallas import tpu as pltpu
from jax.sharding import Mesh
from jax.sharding import PartitionSpec as P


SEQ = ("zl", "y", "x")
SECTION = ("zh", "co")
C = 1536
HALF = C // 2
TAPS = 5
RUN = 1024
EDGE = 12
BLOCK = 96
SHIFTS = (0, 1, -1, 2)
TILES = HALF // 128
GELU = 0.7978845608028654
GRANT = pltpu.CompilerParams(vmem_limit_bytes=24 << 20)


def up16(rows):
    return -(-rows // 16) * 16


def even_chunk(rows, most):
    total = up16(rows)
    return next(total // n for n in range(1, 99) if total % (16 * n) == 0 and total // n <= most)


def activate(load, par_ref, a_scr, rows, edge, meta_ref):
    def step(i, carry):
        start = pl.multiple_of(i * 16, 16)
        parts = load(start)
        squares = jnp.sum(parts[0] * parts[0] + parts[1] * parts[1], axis=-1, keepdims=True)
        scale = lax.rsqrt(squares * (1.0 / C) + 1e-06)
        for side, part in enumerate(parts):
            value = part * scale * par_ref[0:1, side * HALF : (side + 1) * HALF]
            bent = jnp.tanh(value * (GELU + (GELU * 0.044715) * (value * value)))
            half = 0.5 * value
            value = (half + half * bent).astype(jnp.bfloat16).astype(jnp.float32)
            for t in range(TILES):
                tile = value[:, 128 * t : 128 * t + 128]
                a_scr[side * TILES + t, pl.ds(start + 8, 16)] = tile
        return carry

    count = up16(rows) // 16
    lax.fori_loop(0, count, step, 0, unroll=next(n for n in (11, 9, 6, 3, 1) if count % n == 0))

    @pl.when(meta_ref[1] == 1)
    def _():
        for t in range(2 * TILES):
            a_scr[t, 8 : 8 + edge] = jnp.zeros((edge, 128), jnp.float32)

    @pl.when(meta_ref[2] == 1)
    def _():
        for t in range(2 * TILES):
            a_scr[t, 8 + rows - edge : 8 + rows] = jnp.zeros((edge, 128), jnp.float32)


def spread(par_ref, a_scr, d_ref, rows):
    chunk = even_chunk(rows, 176)
    for t in range(2 * TILES):
        lanes = slice(128 * t, 128 * t + 128)
        taps = [par_ref[1 + k : 2 + k, lanes] for k in range(TAPS)]

        def step(i, carry):
            start = pl.multiple_of(i * chunk, 16)
            total = taps[0] * a_scr[t, pl.ds(start + 4, chunk)]
            for k in range(1, TAPS):
                total = total + taps[k] * a_scr[t, pl.ds(start + 4 + 2 * k, chunk)]
            d_ref[pl.ds(start, chunk), lanes] = total.astype(jnp.bfloat16)
            return carry

        lax.fori_loop(0, up16(rows) // chunk, step, 0)


def weight_copies(slot, meta_ref, pieces, w_ref, sems, before=0):
    copies = []
    for piece in pieces:
        for k in range(4):
            n = len(copies)
            row = pl.multiple_of(meta_ref[3 + before + n] * BLOCK, 16)
            source = piece.at[k, slot] if len(piece.shape) == 4 else piece.at[k]
            copies.append(
                pltpu.make_async_copy(source, w_ref.at[pl.ds(row, BLOCK)], sems.at[n])
            )
    return copies


def mix_and_pool(d_ref, w_ref, residual, y_scr, out_ref, rows):
    count = (rows - 8) // 2
    total = up16(rows)
    chunk = even_chunk(rows, 528)
    for start in range(0, total, chunk):
        product = jnp.dot(
            d_ref[start : start + chunk], w_ref[...], preferred_element_type=jnp.float32
        )
        mixed = residual(start, chunk) + product
        for n in range(TILES):
            y_scr[n, start : start + chunk] = mixed[:, 128 * n : 128 * n + 128]
    part = next(p for p in (128, 104, 64, 40, 16, 8, 4) if count % p == 0)
    for start in range(0, count, part):
        for n in range(TILES):
            even = y_scr[n, pl.ds(4 + 2 * start, part, stride=2)]
            odd = y_scr[n, pl.ds(5 + 2 * start, part, stride=2)]
            pooled = jnp.maximum(even, odd).astype(jnp.bfloat16)
            out_ref[start : start + part, 128 * n : 128 * n + 128] = pooled


def first_half(rows, meta_ref, hot_ref, stem_ref, par_ref, x_ref, d_ref, x_scr, a_scr):
    chunk = 176
    for start in range(0, up16(rows), chunk):
        for side, target in enumerate((x_ref, x_scr)):
            target[start : start + chunk] = jnp.dot(
                hot_ref[start : start + chunk],
                stem_ref[:, side * HALF : (side + 1) * HALF],
                preferred_element_type=jnp.float32,
            ).astype(jnp.bfloat16)

    def load(start):
        return [ref[pl.ds(start, 16)].astype(jnp.float32) for ref in (x_ref, x_scr)]

    activate(load, par_ref, a_scr, rows, EDGE, meta_ref)
    spread(par_ref, a_scr, d_ref, rows)


def second_half(rows, meta_ref, x_hbm, d_hbm, *refs):
    _, piece, out_ref, w_ref, x_scr, d_scr, y_scr, sems, row_sems = refs
    copies = weight_copies(0, meta_ref, [piece], w_ref, sems, 12)
    copies.append(pltpu.make_async_copy(d_hbm, d_scr, row_sems.at[0]))
    copies.append(pltpu.make_async_copy(x_hbm, x_scr, row_sems.at[1]))
    for copy in copies:
        copy.start()
    for copy in copies:
        copy.wait()

    def residual(start, chunk):
        return x_scr[start : start + chunk].astype(jnp.float32)

    mix_and_pool(d_scr, w_ref, residual, y_scr, out_ref, rows)


def assemble(slot, meta_ref, *refs):
    *pieces, w_ref, sems = refs
    copies = weight_copies(slot, meta_ref, pieces, w_ref, sems)
    for copy in copies:
        copy.start()
    for copy in copies:
        copy.wait()


def swapped_level(
    rows, edge, meta_ref, own_ref, other_ref, par_ref, w_ref, out_ref, a_scr, d_scr, y_scr
):
    def load(start):
        return [ref[pl.ds(start, 16)].astype(jnp.float32) for ref in (own_ref, other_ref)]

    activate(load, par_ref, a_scr, rows, edge, meta_ref)
    spread(par_ref, a_scr, d_scr, rows)

    def residual(start, chunk):
        return own_ref[start : start + chunk].astype(jnp.float32)

    mix_and_pool(d_scr, w_ref, residual, y_scr, out_ref, rows)


def paired_level(rows, edge, meta_ref, x_ref, par_ref, w_ref, out_ref, a_scr, d_scr, y_scr):
    own = meta_ref[0]

    def load(start):
        return [x_ref[side, pl.ds(start, 16)].astype(jnp.float32) for side in (own, 1 - own)]

    activate(load, par_ref, a_scr, rows, edge, meta_ref)
    spread(par_ref, a_scr, d_scr, rows)

    def residual(start, chunk):
        return x_ref[own, start : start + chunk].astype(jnp.float32)

    mix_and_pool(d_scr, w_ref, residual, y_scr, out_ref, rows)


def spec(memory_space=pltpu.VMEM):
    return pl.BlockSpec(memory_space=memory_space)


def out_rows(rows, last):
    return (rows - 8) // 2 if last else up16((rows - 8) // 2)


def scratch(rows, names):
    size = up16(rows)
    shapes = {
        "a": pltpu.VMEM((2 * TILES, size + 16, 128), jnp.float32),
        "d": pltpu.VMEM((size, C), jnp.bfloat16),
        "x": pltpu.VMEM((size, HALF), jnp.bfloat16),
        "y": pltpu.VMEM((TILES, size, 128), jnp.float32),
        "s": pltpu.SemaphoreType.DMA((16,)),
        "r": pltpu.SemaphoreType.DMA((2,)),
    }
    return [shapes[name] for name in names]


def half_rows(size, width=HALF):
    return jax.ShapeDtypeStruct((size, width), jnp.bfloat16)


def run_first_half(rows, meta, hot, stem, par):
    size = up16(rows)
    return pl.pallas_call(
        lambda *refs: first_half(rows, *refs),
        in_specs=[spec(pltpu.SMEM), spec(), spec(), spec()],
        out_specs=[spec(), spec()],
        out_shape=[half_rows(size), half_rows(size, C)],
        scratch_shapes=scratch(rows, "xa"),
        name="stem_and_taps",
    )(meta, hot, stem, par)


def run_second_half(rows, meta, x, d, begun, piece):
    return pl.pallas_call(
        lambda *refs: second_half(rows, *refs),
        in_specs=[spec(pltpu.SMEM), spec(pltpu.HBM), spec(pltpu.HBM), spec(), spec(pl.ANY)],
        out_specs=[spec(), spec()],
        out_shape=[half_rows(out_rows(rows, False)), half_rows(C)],
        scratch_shapes=scratch(rows, "xdysr"),
        input_output_aliases={3: 1},
        compiler_params=GRANT,
        name="mix_first",
    )(meta, *(pltpu.with_memory_space_constraint(part, pltpu.HBM) for part in (x, d)), begun, piece)


def run_assemble(slot, meta, pieces):
    return pl.pallas_call(
        lambda *refs: assemble(slot, *refs),
        in_specs=[spec(pltpu.SMEM)] + [spec(pl.ANY)] * len(pieces),
        out_specs=spec(),
        out_shape=half_rows(C),
        scratch_shapes=scratch(16, "s"),
        compiler_params=GRANT,
        name="assemble",
    )(meta, *pieces)


def run_swapped_level(rows, edge, meta, own, other, par, weights):
    return pl.pallas_call(
        lambda *refs: swapped_level(rows, edge, *refs),
        in_specs=[spec(pltpu.SMEM)] + [spec()] * 4,
        out_specs=spec(),
        out_shape=half_rows(out_rows(rows, True)),
        scratch_shapes=scratch(rows, "ady"),
        compiler_params=GRANT,
    )(meta, own, other, par, weights)


def run_level(rows, edge, last, meta, x, par, weights):
    return pl.pallas_call(
        lambda *refs: paired_level(rows, edge, *refs),
        in_specs=[spec(pltpu.SMEM)] + [spec()] * 3,
        out_specs=spec(),
        out_shape=half_rows(out_rows(rows, last)),
        scratch_shapes=scratch(rows, "ady"),
        compiler_params=GRANT,
    )(meta, x, par, weights)


def ring(size, by):
    return [(i, (i + by) % size) for i in range(size)]


def around_y(array):
    copies = lax.optimization_barrier(jnp.broadcast_to(array[None], (4, *array.shape)))
    return lax.all_to_all(copies, "y", 0, 0, tiled=True)


def own_first(array, co):
    turned = jnp.concatenate([array[..., HALF:], array[..., :HALF]], axis=-1)
    return jnp.where(co == 0, array, turned)


def flat(b, g, role):
    zh, zl, y = 2 * b + g % 2, g // 8, (g // 2) % 4
    return ((zh * 4 + zl) * 4 + y) * 4 + role


def gathered_bases(bases, sequence):
    mine = lax.dynamic_index_in_dim(bases + 1, sequence, 0, keepdims=False)
    parts = []
    for by in (-1, 0, 1, 2):
        pairs = []
        for zh in range(4):
            for row in range(16):
                place = 4 * row + 2 * (zh % 2) + by
                if 0 <= place < 64:
                    pairs.append((zh * 64 + place, zh * 64 + row * 4))
        parts.append(lax.ppermute(mine, ("zh", "zl", "y", "x"), pairs))
    return parts


def pass_on(array, role):
    rows = array.shape[0]
    axes = ("zh", "zl", "y", "x")
    up = [(flat(b, g, role), flat(b, g + 1, role + 1)) for b in range(2) for g in range(31)]
    down = [(flat(b, g + 1, role), flat(b, g, role + 1)) for b in range(2) for g in range(31)]
    before = lax.ppermute(array[rows - EDGE :], axes, up)
    after = lax.ppermute(array[:EDGE], axes, down)
    own = lax.ppermute(array, "x", [(role, role + 1)])
    blank = jnp.zeros((8, HALF), array.dtype)
    return jnp.concatenate([before, own, after, blank], axis=0)


def relay(bases, stem_weight, gains, depth_taps, point_weight):
    zh, co, zl, y, x = [lax.axis_index(name) for name in ("zh", "co", "zl", "y", "x")]
    margin = stem_weight.shape[0] // 2
    group = (zl * 4 + y) * 2 + zh % 2
    sequence = zh // 2

    held = [point_weight[0], gains, depth_taps[0], jnp.zeros((2, C), gains.dtype)]
    held = lax.all_gather(jnp.concatenate(held, axis=0), "zh")
    held, bases = lax.optimization_barrier((held, bases))
    ids = gathered_bases(bases, sequence)
    blocks = held[:, :24].reshape(4, 24, 2, HALF).transpose(2, 0, 1, 3)
    blocks = jnp.broadcast_to(blocks[:, None], (2, 4, 4, 24, HALF)).reshape(32, 24, HALF)
    blocks = lax.optimization_barrier(blocks)
    blocks = lax.all_to_all(blocks, ("co", "y", "x"), 0, 0, tiled=True)
    near = lax.optimization_barrier(blocks.reshape(2, 4, BLOCK, HALF))
    share = lax.dynamic_index_in_dim(near, y, 1, keepdims=False)
    share0 = lax.ppermute(share[0], ("zh", "zl"), ring(16, 2))
    share1 = lax.ppermute(share[1], ("zh", "zl"), ring(16, -2))
    beside = []
    for slot in range(2):
        sides = [near[slot]]
        for by in (1, -1):
            sides.append(lax.ppermute(near[slot], ("zh", "zl"), ring(16, by)))
        beside.append(sides)
    opposite = around_y(jnp.stack([share0, share1]))
    pieces = [sides + [opposite] for sides in beside]
    params = lax.dynamic_index_in_dim(held, x, 0, keepdims=False)[24:]
    params = lax.all_gather(params, "co")
    params = own_first(params, co).astype(jnp.float32)
    four = jnp.arange(4, dtype=jnp.int32)
    z_of = (zl - jnp.array(SHIFTS, jnp.int32)) % 4
    place = (z_of[:, None] * 4 + four[None, :]).reshape(-1)
    flags = jnp.stack([co, (group == 0).astype(jnp.int32), (group == 31).astype(jnp.int32)])
    meta = jnp.concatenate([flags.astype(jnp.int32), (place + 8 * co) % 16])

    rows = RUN + 2 * EDGE
    size = up16(rows)
    ids = jnp.concatenate(ids)[bases.shape[1] - EDGE - margin :][: size + 2 * margin]
    windows = jnp.stack([ids[k : k + size] for k in range(2 * margin + 1)])
    kinds = jnp.arange(1, 5, dtype=jnp.int32)[None, :, None]
    hot = (windows[:, None, :] == kinds).astype(jnp.bfloat16).reshape(-1, size)
    hot = jnp.pad(hot, ((0, 4), (0, 0))).T
    stem = own_first(jnp.pad(stem_weight.reshape(-1, C), ((0, 4), (0, 0))), co)
    level_rows, taps = run_first_half(rows, meta, hot, stem, params[0])
    begun = run_assemble(0, meta, pieces[0][:3])
    now, even_weights = run_second_half(rows, meta, level_rows, taps, begun, pieces[0][3])
    other = lax.ppermute(now, "co", [(0, 1), (1, 0)])
    odd_weights = run_assemble(1, meta, pieces[1])
    now = run_swapped_level(RUN // 2 + 8, 4, meta, now, other, params[1], odd_weights)
    run = RUN // 4
    for role in range(3):
        now = lax.all_gather(pass_on(now, role), "co")
        now = run_level(run + 2 * EDGE, EDGE, False, meta, now, params[0], even_weights)
        now = lax.all_gather(now, "co")
        now = run_level(run // 2 + 8, 4, True, meta, now, params[1], odd_weights)
        run = run // 4

    kept = jnp.zeros((2, HALF), now.dtype)
    for k in range(2):
        for p in range(2):
            pairs = [
                (((2 * b + h) * 2 + c) * 4 + 3, ((2 * c + k) * 2 + b) * 4 + 2 * h + p)
                for b in range(2)
                for h in range(2)
                for c in range(2)
            ]
            kept = kept + lax.ppermute(now[2 * p : 2 * p + 2], ("zh", "co", "x"), pairs)
    kept = lax.all_gather(kept, "co").reshape(2, 2, 4, HALF // 4)
    return lax.dynamic_index_in_dim(kept, (zh % 2) * 2 + co, 2, keepdims=False)


def solution(mesh):
    finer = Mesh(mesh.devices.reshape(4, 2, 4, 4, 4), SECTION + SEQ)
    in_specs = (
        P(None, SEQ),
        P(),
        P(SECTION, None),
        P(SECTION, None, None),
        P(SECTION, SEQ, None),
    )
    out_specs = P(None, SEQ, SECTION)
    return jax.shard_map(relay, mesh=finer, in_specs=in_specs, out_specs=out_specs, check_vma=False)
```
